128 devices in a mesh: rows: 32 (over y, x, core), tm: 4 (over z).
Axes of the slice: x: 4, y: 4, z: 4, core: 2. Of those that a mesh axis runs over, the one named last changes fastest.
Arguments:
- snapshots: bfloat16 [524288, 512], P('rows', 'tm'), may hold values from -170 to 170, as said below
- lift: bfloat16 [512, 384], replicated, may hold values from -0.3125 to 0.3125
- adjacency: int32 [1024, 6], P(('rows', 'tm')), may hold values from -1 to 1023, as said below
- codes: int32 [1024, 6], P(('rows', 'tm')), may hold values from 0 to 3, as said below
- obstacle: int32 [1024], P(('rows', 'tm')), may hold values 0 or 1
Outputs:
- modes: float32 [524288, 512], P(('rows', 'tm'))
- rfactor: float32 [512, 512], replicated
The draws below stay inside these ranges and needn't reach their ends.
Inputs may be any that keep to these rules, and one draw needn't show every extreme that they name: `snapshots`: custom float draw with element and snapshot scales. `adjacency`: the layer of an element is its index // 8. The -z and +z neighbours lie in the layers below and above, cyclic over 128 layers; the x and y neighbours lie in the element's own layer; -1 stands only on -y or +y faces. Neighbours are mutual: e lies beyond face f xor 1 of the element beyond its face f. Quarter turns of the neighbour's face nodes; the two codes of a shared face add up to a multiple of 4; 0 on walls.
All inputs are finite; a program needn't handle non-finite values. No bound on the sum of `obstacle` on one device may be relied on, other than what follows from the above.
Results may differ from the reference program's by a relative error of at most 0.0041.
Values may be sent and summed in bfloat16 or wider, within the bound.
A program may use at most 128 MiB of HBM per device.

```python
import math
import jax
import jax.numpy as jnp
from jax import lax

P_SIZE = 8
NODES = 512
FACE = 64
S = 512
E_DEV = 8
NZL = 128
ELEMS = 1024
ROWS_ALL = 524288


def draw_snapshots(key, part):
    elem_scale = jnp.exp(jax.random.uniform(jax.random.fold_in(key, 2), (ELEMS,), jnp.float32, math.log(0.3), math.log(3.0)))
    layer_pos = (jnp.arange(ELEMS) // E_DEV).astype(jnp.float32)
    rising = 1.0 + 2.0 * layer_pos / (NZL - 1)
    col_scale = jnp.exp(jax.random.uniform(jax.random.fold_in(key, 3), (S,), jnp.float32, math.log(0.3), math.log(3.0)))
    row_scale = jnp.repeat(elem_scale * rising, NODES)
    values = jnp.clip(jax.random.normal(jax.random.fold_in(key, 1), (ROWS_ALL, S), jnp.float32), -6.0, 6.0)
    return (row_scale[:, None] * values * col_scale[None, :]).astype(jnp.bfloat16)


def mesh_tables(key):
    across = E_DEV // 2
    position = jnp.arange(E_DEV, dtype=jnp.int32)
    column_x = position // 2
    column_y = position % 2
    layer_keys = jax.random.split(jax.random.fold_in(key, 21), NZL)
    orders = jax.vmap(lambda sub_key: jax.random.permutation(sub_key, E_DEV))(layer_keys).astype(jnp.int32)
    layer_ids = jnp.arange(NZL, dtype=jnp.int32)[:, None]
    global_ids = layer_ids * E_DEV + orders
    minus_x = jnp.mod(column_x - 1, across) * 2 + column_y
    plus_x = jnp.mod(column_x + 1, across) * 2 + column_y
    minus_y = jnp.clip(position - 1, 0, E_DEV - 1)
    plus_y = jnp.clip(position + 1, 0, E_DEV - 1)
    walls = jnp.full((NZL, E_DEV), -1, jnp.int32)
    neighbours = jnp.stack([global_ids[:, minus_x], global_ids[:, plus_x], jnp.where(column_y == 1, global_ids[:, minus_y], walls), jnp.where(column_y == 0, global_ids[:, plus_y], walls), jnp.roll(global_ids, 1, axis=0), jnp.roll(global_ids, -1, axis=0)], axis=-1)
    turns = jax.random.randint(jax.random.fold_in(key, 22), (NZL, E_DEV, 3), 0, 4).astype(jnp.int32)
    zeros = jnp.zeros((NZL, E_DEV), jnp.int32)
    code_grid = jnp.stack([jnp.mod(4 - turns[:, minus_x, 0], 4), turns[:, :, 0], jnp.where(column_y == 1, jnp.mod(4 - turns[:, minus_y, 1], 4), zeros), jnp.where(column_y == 0, turns[:, :, 1], zeros), jnp.mod(4 - jnp.roll(turns[:, :, 2], 1, axis=0), 4), turns[:, :, 2]], axis=-1)
    inverse = jnp.argsort(orders, axis=1, stable=True).astype(jnp.int32)
    adjacency = jnp.take_along_axis(neighbours, inverse[:, :, None], axis=1).reshape(ELEMS, 6)
    codes = jnp.take_along_axis(code_grid, inverse[:, :, None], axis=1).reshape(ELEMS, 6)
    return (adjacency, codes)


def draw_adjacency(key, part):
    return mesh_tables(jax.random.fold_in(key, 20))[0]


def draw_codes(key, part):
    return mesh_tables(jax.random.fold_in(key, 20))[1]


def with_ends(result, own_key, least, top_value):
    shape = result.shape
    index_at = [jax.random.randint(jax.random.fold_in(own_key, axis), (), 0, shape[axis]) for axis in range(len(shape))]
    result = result.at[tuple(index_at)].set(least)
    longest = shape.index(max(shape))
    index_at[longest] = (index_at[longest] + 1) % shape[longest]
    return result.at[tuple(index_at)].set(top_value)


def normal_values(key, dims, scale, reach, kind=jnp.bfloat16):
    drawn = jax.random.normal(key, dims, jnp.float32) * scale
    return jnp.minimum(jnp.maximum(drawn, -reach), reach).astype(kind)


def setup_inputs(seed: int = 0) -> dict:
    key_of = jax.random.split(jax.random.key(seed), 6)
    snapshots = draw_snapshots(jax.random.fold_in(key_of[5], 71), 0)
    lift = normal_values(key_of[1], (NODES, 6 * FACE), (6 * FACE) ** -0.5, 0.3125)
    adjacency = draw_adjacency(jax.random.fold_in(key_of[5], 71), 0)
    codes = draw_codes(jax.random.fold_in(key_of[5], 71), 0)
    obstacle = with_ends((jax.random.randint(key_of[4], (ELEMS,), 0, 4) < 1).astype(jnp.int32), jax.random.fold_in(key_of[4], 1), 0, 1)
    return {"snapshots": snapshots, "lift": lift, "adjacency": adjacency, "codes": codes, "obstacle": obstacle}


def face_traces(nodal_block, per_side):
    final = per_side - 1
    return jnp.stack([nodal_block[:, 0], nodal_block[:, final], nodal_block[:, :, 0], nodal_block[:, :, final], nodal_block[:, :, :, 0], nodal_block[:, :, :, final]], axis=1)

def weigh_layers(nodal_block, adjacency, codes, obstacle, lower_five, upper_four, first_elem, elem_total, lift):
    elements = nodal_block.shape[0]
    per_side = nodal_block.shape[1]
    columns = nodal_block.shape[-1]
    per_layer = lower_five.shape[0]
    traces = face_traces(nodal_block, per_side)
    own_offset = jnp.mod(adjacency - first_elem, elem_total).astype(jnp.int32)
    low_offset = jnp.mod(adjacency - first_elem + per_layer, elem_total).astype(jnp.int32)
    tables = (traces[:, 1], traces[:, 0], traces[:, 3], traces[:, 2], jnp.concatenate([lower_five, traces[:, 5]], 0), jnp.concatenate([traces[:, 4], upper_four], 0))
    offsets = (own_offset, own_offset, own_offset, own_offset, low_offset, own_offset)
    picked = jnp.stack([jnp.take(tables[face_id], jnp.clip(offsets[face_id][:, face_id], 0, tables[face_id].shape[0] - 1), axis=0) for face_id in range(6)], axis=1).astype(jnp.float32)
    turned = jnp.zeros_like(picked)
    for quarter in range(4):
        matches = (codes == quarter)[:, :, None, None, None]
        turned = jnp.where(matches, jnp.rot90(picked, quarter, axes=(2, 3)), turned)
    turned = jnp.where((adjacency >= 0)[:, :, None, None, None], turned, 0.0)
    face_jumps = (turned - traces.astype(jnp.float32)).astype(jnp.bfloat16).reshape(elements, -1, columns)
    lifted = jnp.einsum('nk,eks->ens', lift.astype(jnp.float32), face_jumps.astype(jnp.float32), precision=lax.Precision.HIGHEST)
    damping = 1.0 - 0.5 * obstacle.astype(jnp.float32)
    return damping[:, None, None] * nodal_block.reshape(elements, -1, columns).astype(jnp.float32) + lifted

def reference(snapshots, lift, adjacency, codes, obstacle):
    stacked = snapshots.reshape(NZL, E_DEV, P_SIZE, P_SIZE, P_SIZE, S)
    adjacency_layers = adjacency.reshape(NZL, E_DEV, 6)
    codes_layers = codes.reshape(NZL, E_DEV, 6)
    obstacle_layers = obstacle.reshape(NZL, E_DEV)

    def one_layer(gram_sum, layer_id):
        nodal_block = stacked[layer_id]
        lower_five = stacked[jnp.mod(layer_id - 1, NZL)][:, :, :, P_SIZE - 1]
        upper_four = stacked[jnp.mod(layer_id + 1, NZL)][:, :, :, 0]
        weighted = weigh_layers(nodal_block, adjacency_layers[layer_id], codes_layers[layer_id], obstacle_layers[layer_id], lower_five, upper_four, layer_id * E_DEV, ELEMS, lift)
        weighted = weighted.reshape(E_DEV * NODES, S).astype(jnp.bfloat16)
        wide = weighted.astype(jnp.float32)
        gram_part = jnp.einsum('rs,rt->st', wide, wide, precision=lax.Precision.HIGHEST) / ROWS_ALL
        return (gram_sum + gram_part, weighted)
    gram, weighted_all = lax.scan(one_layer, jnp.zeros((S, S), jnp.float32), jnp.arange(NZL, dtype=jnp.int32))
    lower_factor = jnp.linalg.cholesky(gram)

    def solve_layer(weighted):
        return jax.scipy.linalg.solve_triangular(lower_factor, weighted.astype(jnp.float32).T, lower=True).T
    modes = lax.map(solve_layer, weighted_all).reshape(ROWS_ALL, S)
    return (modes, lower_factor.T)
```

```python
import math

import jax
import jax.numpy as jnp
from jax import lax
from jax.sharding import Mesh
from jax.sharding import PartitionSpec as P
from jax.experimental import pallas as pl
from jax.experimental.pallas import tpu as pltpu

ROWS = ("rows_0", "rows_1", "rows_2")
ROWS_TM = ("rows_0", "rows_1", "rows_2", "tm")


def extended(x, sides, width):
    edges = {}
    for axis, dim in sides:
        peers, length = (lax.axis_size(axis), x.shape[dim])
        up = [(i, (i + 1) % peers) for i in range(peers)]
        last = lax.slice_in_dim(x, length - width, length, axis=dim)
        leading = lax.slice_in_dim(x, 0, width, axis=dim)
        edges[dim] = (
            lax.ppermute(last, axis, up),
            lax.ppermute(leading, axis, [(b, a) for a, b in up]),
        )
    done = []
    for _, dim in sides:
        low, high = edges[dim]
        around = [(width, width) if d in done else (0, 0) for d in range(x.ndim)]
        x = jnp.concatenate([jnp.pad(low, around), x, jnp.pad(high, around)], axis=dim)
        done.append(dim)
    return x


def in_blocks(x, dim, peers):
    lengths = x.shape
    tiles = x.reshape(*lengths[:dim], peers, lengths[dim] // peers, *lengths[dim + 1 :])
    return jnp.moveaxis(tiles, dim, 0)


def sum_at_owner(x, axis, dim):
    tiles = in_blocks(x, dim, lax.axis_size(axis))
    arrived = lax.all_to_all(tiles, axis, split_axis=0, concat_axis=0, tiled=True)
    return arrived.sum(axis=0)


def sum_by_axis(x, axes, dim):
    far, near = axes
    own = sum_at_owner(in_blocks(x, dim, lax.axis_size(far)), near, dim + 1)
    return jnp.sum(lax.all_to_all(own, far, 0, 0, tiled=True), axis=0)


def rows_for(lines, peers):
    spare = -lines.shape[0] % peers
    if not spare:
        return lines
    return jnp.concatenate([lines, jnp.zeros((spare, *lines.shape[1:]), lines.dtype)])


def sent_to_all(x, axis):
    copies = jnp.broadcast_to(x, (lax.axis_size(axis), *x.shape))
    return lax.all_to_all(copies, axis, split_axis=0, concat_axis=0, tiled=True)


def laid_out(tiles, dim):
    tiles = jnp.moveaxis(tiles, 0, dim)
    lengths = tiles.shape
    return tiles.reshape(*lengths[:dim], lengths[dim] * lengths[dim + 1], *lengths[dim + 2 :])


def whole_of(x, axes, dim):
    far, near = axes
    leading = sent_to_all(x, far)
    tiles = jnp.swapaxes(sent_to_all(leading, near), 0, 1)
    return laid_out(tiles.reshape(-1, *x.shape), dim)


def sum_by_parts(x, axes):
    lines = x.reshape(-1, x.shape[-1])
    own = sum_by_axis(rows_for(lines, lax.axis_size(axes[0]) * lax.axis_size(axes[1])), axes, 0)
    whole = whole_of(own, axes, 0)
    return whole[: len(lines)].reshape(x.shape)


def face_traces(nodal_block, per_side):
    final = per_side - 1
    return jnp.stack(
        [
            nodal_block[:, 0],
            nodal_block[:, final],
            nodal_block[:, :, 0],
            nodal_block[:, :, final],
            nodal_block[:, :, :, 0],
            nodal_block[:, :, :, final],
        ],
        axis=1,
    )


def weigh_layers(
    nodal_block, adjacency, codes, obstacle, lower_five, upper_four, first_elem, elem_total, lift
):
    elements = nodal_block.shape[0]
    per_side = nodal_block.shape[1]
    columns = nodal_block.shape[-1]
    per_layer = lower_five.shape[0]
    traces = face_traces(nodal_block, per_side)
    own_offset = jnp.mod(adjacency - first_elem, elem_total)
    low_offset = jnp.mod(adjacency - first_elem + per_layer, elem_total)
    tables = (
        traces[:, 1],
        traces[:, 0],
        traces[:, 3],
        traces[:, 2],
        jnp.concatenate([lower_five, traces[:, 5]], 0),
        jnp.concatenate([traces[:, 4], upper_four], 0),
    )
    offsets = (own_offset, own_offset, own_offset, own_offset, low_offset, own_offset)
    picked = jnp.stack(
        [
            jnp.take(
                tables[face_id],
                jnp.clip(offsets[face_id][:, face_id], 0, tables[face_id].shape[0] - 1),
                axis=0,
            )
            for face_id in range(6)
        ],
        axis=1,
    ).astype(jnp.float32)
    turned = jnp.zeros_like(picked)
    for quarter in range(4):
        matches = (codes == quarter)[:, :, None, None, None]
        turned = jnp.where(matches, jnp.rot90(picked, quarter, axes=(2, 3)), turned)
    turned = jnp.where((adjacency >= 0)[:, :, None, None, None], turned, 0.0)
    face_jumps = (
        (turned - traces.astype(jnp.float32)).astype(jnp.bfloat16).reshape(elements, -1, columns)
    )
    lifted = jnp.einsum("nk,eks->ens", lift, face_jumps, preferred_element_type=jnp.float32)
    damping = 1.0 - 0.5 * obstacle.astype(jnp.float32)
    weighted = (
        damping[:, None, None] * nodal_block.reshape(elements, -1, columns).astype(jnp.float32)
        + lifted
    )
    return weighted.astype(jnp.bfloat16)


F32 = jnp.float32
BF = jnp.bfloat16
HI = lax.Precision.HIGHEST


def lanes_of(x, lane):
    return jnp.broadcast_to(x[:, lane : lane + 1], x.shape)


def row_of(x, row):
    return jnp.broadcast_to(x[row : row + 1, :], x.shape)


def factor_block(a, e):
    tiles = len(a)
    sub = lax.broadcasted_iota(jnp.int32, (8, 128), 0)
    upper, inverse = [], []
    for p in range(tiles):
        s = 8 * p
        c = [lanes_of(a[p], s + j) for j in range(8)]
        pa, pe = a[p], e[p]
        ra, re = pa, pe
        for j in range(8):
            d = row_of(c[j], j)
            inv = 1.0 / d
            scale = lax.rsqrt(d)
            here = sub == j
            m = jnp.where(here, -inv, c[j] * inv)
            qa, qe = row_of(pa, j), row_of(pe, j)
            ra = jnp.where(here, qa * scale, ra)
            re = jnp.where(here, qe * scale, re)
            pa = jnp.where(here, 0.0, pa) - m * qa
            pe = jnp.where(here, 0.0, pe) - m * qe
            for k in range(j + 1, 8):
                ck = row_of(c[k], j)
                c[k] = jnp.where(here, 0.0, c[k]) - m * ck
        upper.append(ra)
        inverse.append(re)
        qa = [row_of(pa, j) for j in range(8)]
        qe = [row_of(pe, j) for j in range(8)]
        for i in range(p + 1, tiles):
            l = [lanes_of(a[i], s + j) for j in range(8)]
            ua = [l[j] * qa[j] for j in range(8)]
            ue = [l[j] * qe[j] for j in range(8)]
            a[i] = a[i] - (((ua[0] + ua[1]) + (ua[2] + ua[3])) + ((ua[4] + ua[5]) + (ua[6] + ua[7])))
            e[i] = e[i] - (((ue[0] + ue[1]) + (ue[2] + ue[3])) + ((ue[4] + ue[5]) + (ue[6] + ue[7])))
    return upper, inverse


def chol_kernel(g_ref, w_ref, modes_ref, r_ref, work, inv_hi, inv_lo, stage, sem):
    n = g_ref.shape[0]
    blocks = n // 128
    rows = w_ref.shape[0]
    work[:, 0:n] = g_ref[...]
    work[:, n : 2 * n] = jnp.zeros((n, n), F32)
    sub = lax.broadcasted_iota(jnp.int32, (8, 128), 0)
    lane = lax.broadcasted_iota(jnp.int32, (8, 128), 1)

    def out_copy(kb):
        slot = lax.rem(kb, 2)
        return pltpu.make_async_copy(
            stage.at[slot], modes_ref.at[:, pl.ds(pl.multiple_of(kb * 128, 128), 128)], sem.at[slot]
        )

    @pl.loop(0, blocks)
    def _(kb):
        r0 = pl.multiple_of(kb * 128, 128)
        a = [work[pl.ds(pl.multiple_of(r0 + 8 * i, 8), 8), pl.ds(r0, 128)] for i in range(16)]
        e = [jnp.where(lane == sub + 8 * i, 1.0, 0.0) for i in range(16)]
        upper, inverse = factor_block(a, e)
        for i in range(16):
            work[pl.ds(pl.multiple_of(r0 + 8 * i, 8), 8), pl.ds(r0, 128)] = upper[i]
            work[pl.ds(pl.multiple_of(r0 + 8 * i, 8), 8), pl.ds(pl.multiple_of(r0 + n, 128), 128)] = inverse[i]
        own = pl.ds(r0, 128)
        linv = work[own, pl.ds(pl.multiple_of(r0 + n, 128), 128)]
        rest = pl.ds(pl.multiple_of(r0 + 128, 128), n - 128)
        work[own, rest] = jnp.dot(linv, work[own, rest], precision=HI, preferred_element_type=F32)

        @pl.loop(kb + 1, blocks)
        def _(i):
            ri = pl.multiple_of(i * 128, 128)
            left = work[own, pl.ds(ri, 128)].T
            window = pl.ds(pl.multiple_of(r0 + 128, 128), n)
            work[pl.ds(ri, 128), window] = work[pl.ds(ri, 128), window] - jnp.dot(
                left, work[own, window], precision=HI, preferred_element_type=F32
            )

        row = work[own, pl.ds(n, n)]
        hi = row.astype(BF)
        inv_hi[...] = hi
        inv_lo[...] = (row - hi.astype(F32)).astype(BF)

        @pl.when(kb >= 2)
        def _():
            out_copy(kb - 2).wait()

        slot = lax.rem(kb, 2)
        NT = (((1,), (1,)), ((), ()))

        @pl.loop(0, rows // 512)
        def _(q):
            part = pl.ds(pl.multiple_of(q * 512, 512), 512)
            x = w_ref[part, :]
            stage[slot, part, :] = lax.dot_general(
                x, inv_hi[...], NT, preferred_element_type=F32
            ) + lax.dot_general(x, inv_lo[...], NT, preferred_element_type=F32)

        out_copy(kb).start()

    out_copy(blocks - 2).wait()
    out_copy(blocks - 1).wait()
    ri = lax.broadcasted_iota(jnp.int32, (n, n), 0)
    ci = lax.broadcasted_iota(jnp.int32, (n, n), 1)
    r_ref[...] = jnp.where(ri <= ci, work[:, 0:n], 0.0)


def factor_and_modes(gram, weighted):
    n = gram.shape[0]
    rows = weighted.shape[0]
    vm = pl.BlockSpec(memory_space=pltpu.VMEM)
    return pl.pallas_call(
        chol_kernel,
        name="factor_modes",
        out_shape=(jax.ShapeDtypeStruct((rows, n), F32), jax.ShapeDtypeStruct((n, n), F32)),
        in_specs=[vm, vm],
        out_specs=(pl.BlockSpec(memory_space=pl.ANY), vm),
        scratch_shapes=[
            pltpu.VMEM((n, 2 * n), F32),
            pltpu.VMEM((128, n), BF),
            pltpu.VMEM((128, n), BF),
            pltpu.VMEM((2, rows, 128), F32),
            pltpu.SemaphoreType.DMA((2,)),
        ],
    )(gram, weighted)


def on_device(snapshots, lift, adjacency, codes, obstacle):
    tm_size = lax.axis_size("tm")
    rows_size = lax.axis_size(ROWS)
    face_nodes = lift.shape[1] // 6
    per_side = math.isqrt(face_nodes)
    node_count = lift.shape[0]
    per_layer = adjacency.shape[0]
    elem_total = per_layer * rows_size * tm_size
    regrouped = lax.all_to_all(snapshots, "tm", split_axis=0, concat_axis=1, tiled=True)
    nodal_block = regrouped.reshape(per_layer, per_side, per_side, per_side, -1)
    rim_faces = jnp.stack([nodal_block[:, :, :, 0], nodal_block[:, :, :, per_side - 1]], 0)
    padded = extended(rim_faces, ((ROWS_TM, 0),), 1)
    first_elem = lax.axis_index(ROWS_TM) * per_layer
    weighted = weigh_layers(
        nodal_block, adjacency, codes, obstacle, padded[0], padded[3], first_elem, elem_total, lift
    )
    weighted = weighted.reshape(per_layer * node_count, -1)
    row_total = elem_total * node_count
    gram_local = (
        jnp.einsum("rs,rt->st", weighted, weighted, preferred_element_type=jnp.float32) / row_total
    )
    total_gram = sum_by_parts(gram_local, (("rows_0", "rows_1"), ("rows_2", "tm")))
    return factor_and_modes(total_gram, weighted)


def solution(mesh):
    split = Mesh(
        mesh.devices.reshape(4, 4, 2, mesh.shape["tm"]), ("rows_0", "rows_1", "rows_2", "tm")
    )
    return jax.shard_map(
        on_device,
        mesh=split,
        in_specs=(P(ROWS, "tm"), P(), P(ROWS_TM, None), P(ROWS_TM, None), P(ROWS_TM)),
        out_specs=(P(ROWS_TM, None), P()),
        check_vma=False,
    )
```

```python
import jax
import jax.numpy as jnp
from jax import lax
from jax.experimental import pallas as pl
from jax.experimental.pallas import tpu as pltpu
from jax.sharding import Mesh
from jax.sharding import PartitionSpec as P

ROWS = ("rows_0", "rows_1", "rows_2")
ROWS_TM = ("rows_0", "rows_1", "rows_2", "tm")
HI = lax.Precision.HIGHEST
F32 = jnp.float32
BF = jnp.bfloat16
MESH = pl.DeviceIdType.MESH
NODES = 512
LAYER = 8 * NODES
PAIR = 2 * NODES
TILES = 1280


def at(start, size, step=8):
    return pl.ds(pl.multiple_of(start, step), size)


def halves(face):
    last = face % 2
    if face < 2:
        return last * 448, 8, 1
    if face < 4:
        return last * 56, 64, 1
    return last * 7, 64, 8


def strided(ref, start, step):
    return ref[pl.ds(start, 8), :] if step == 1 else ref[pl.ds(start, 8, stride=step), :]


def weigh_kernel(
    snap_ref, lift_ref, tab_ref, out_ref, gram_ref,
    raw, nodes, sent, whole, tabs, smem_tabs, up_face, down_face, low_halo, high_halo,
    jump, gram, part, core_in, plane_in, z_in,
    load_sem, out_sem, tab_send, tab_recv, smem_sem, halo_send, halo_recv,
    send_sem, recv_sem, own_sem, core_send, core_recv, plane_send, plane_recv,
    z_send, z_recv, back_send, back_recv, pair_send, pair_recv,
):
    y, x, c, t = (lax.axis_index(n) for n in ("rows_0", "rows_1", "rows_2", "tm"))
    r = (y * 4 + x) * 2 + c
    xy = y * 4 + x

    def group(index):
        index = lax.rem(index + 32, 32)
        return (index // 8, lax.rem(index // 2, 4), lax.rem(index, 2), t)

    def plane(index):
        index = lax.rem(index, 16)
        return (index // 4, lax.rem(index, 4), c, t)

    def column(index):
        return (y, x, c, index)

    partner = (y, x, 1 - c, t)
    other = (lambda: group(r + jnp.where(c == 1, 1, -1)))

    def remote(src, dst, send, recv, device):
        return pltpu.make_async_remote_copy(
            src_ref=src, dst_ref=dst, send_sem=send, recv_sem=recv, device_id=device, device_id_type=MESH
        )

    barrier = pltpu.get_barrier_semaphore()
    for o in range(1, 4):
        pl.semaphore_signal(barrier, inc=1, device_id=column(lax.rem(t + o, 4)), device_id_type=MESH)
    pl.semaphore_signal(barrier, inc=1, device_id=partner, device_id_type=MESH)
    pl.semaphore_signal(barrier, inc=1, device_id=other(), device_id_type=MESH)

    @pl.loop(1, 16)
    def _(o):
        pl.semaphore_signal(barrier, inc=1, device_id=plane(xy + o), device_id_type=MESH)

    def load(l):
        rows = at(l * LAYER, LAYER)
        return pltpu.make_async_copy(snap_ref.at[rows, :], raw.at[rows, :], load_sem.at[l])

    for l in (3, 0, 1, 2):
        load(l).start()
    for l in (3, 0, 1, 2):
        load(l).wait()

        @pl.loop(0, LAYER // 128)
        def _(i):
            nodes[at((l + 1) * LAYER + i * 128, 128), :] = raw[at(l * LAYER + i * 128, 128), :].astype(F32)

        if l in (3, 0):
            face, buffer = (7, up_face) if l == 3 else (0, down_face)

            @pl.loop(0, 32)
            def _(i):
                base = (l + 1) * LAYER + i * 128 + face
                two = [nodes[pl.ds(base + 64 * h, 8, stride=8), :] for h in range(2)]
                buffer[at(i * 16, 16, 16), :] = jnp.concatenate(two, axis=0).astype(BF)

    pl.semaphore_wait(barrier, 20)

    def tab_copy(o):
        return remote(tab_ref, tabs.at[t], tab_send.at[o - 1], tab_recv.at[t], column(lax.rem(t + o, 4)))

    for o in range(1, 4):
        tab_copy(o).start()
    up = remote(up_face, low_halo, halo_send.at[0], halo_recv.at[0], group(r + 1))
    down = remote(down_face, high_halo, halo_send.at[1], halo_recv.at[1], group(r - 1))
    up.start()
    down.start()
    mine = pltpu.make_async_copy(tab_ref, tabs.at[t], own_sem.at[4])
    mine.start()
    mine.wait()
    for o in range(1, 4):
        src = lax.rem(t + o, 4)
        remote(tab_ref, tabs.at[src], tab_send.at[o - 1], tab_recv.at[src], column(src)).wait_recv()
    to_smem = pltpu.make_async_copy(tabs, smem_tabs, smem_sem)
    to_smem.start()
    to_smem.wait()

    sub = lax.broadcasted_iota(jnp.int32, (8, 128), 0)

    def split_step(s):
        m = lax.rem(s, 4)
        return s // 4, jnp.where(m == 3, 3, lax.rem(m + 1, 3))

    def layer_copy(q, l):
        return remote(
            sent.at[at(l * LAYER + q * PAIR, PAIR), :],
            whole.at[at(q * PAIR, PAIR), at(t * 128, 128, 128)],
            send_sem.at[l, q], recv_sem.at[t, q], column(l),
        )

    def own_copy(q):
        return pltpu.make_async_copy(
            sent.at[at(t * LAYER + q * PAIR, PAIR), :],
            whole.at[at(q * PAIR, PAIR), at(t * 128, 128, 128)], own_sem.at[q],
        )

    def send_step(s):
        q, l = split_step(s)

        @pl.when(l == t)
        def _():
            own_copy(q).start()

        @pl.when(l != t)
        def _():
            layer_copy(q, l).start()

    @pl.loop(0, 16)
    def _(s):
        q, l = split_step(s)
        slot = lax.rem(s, 2)

        @pl.when(s == 2)
        def _():
            for copy, halo, layer, face in ((up, low_halo, 0, 7), (down, high_halo, 5, 0)):
                copy.wait_recv()

                @pl.loop(0, 32)
                def _(i):
                    two = halo[at(i * 16, 16, 16), :].astype(F32)
                    base = layer * LAYER + i * 128 + face
                    nodes[pl.ds(base, 8, stride=8), :] = two[0:8]
                    nodes[pl.ds(base + 64, 8, stride=8), :] = two[8:16]

        for h in range(2):
            e = 2 * q + h
            own = ((l + 1) * 8 + e) * NODES
            for f in range(6):
                n = smem_tabs[l, e, f]
                k = smem_tabs[l, e, 6 + f]
                shift = (0, 0, 0, 0, -1, 1)[f]
                base = ((l + 1 + shift) * 8 + (n & 7)) * NODES
                turn = jnp.where((k == 1) | (k == 2), 1, 0)
                odd = (k & 1) == 1
                order = jnp.where(k >= 2, 7 - sub, sub)
                wall = n < 0
                nb_first, nb_tile, nb_sub = halves(f ^ 1)
                my_first, my_tile, my_sub = halves(f)
                done = []
                for i in range(8):
                    j = i + turn * (7 - 2 * i)
                    straight = strided(nodes, base + nb_first + j * nb_tile, nb_sub)
                    across = strided(nodes, base + nb_first + j * nb_sub, nb_tile)
                    got = jnp.where(odd, across, straight)
                    got = jnp.take_along_axis(got, order, axis=0)
                    got = jnp.where(wall, 0.0, got)
                    done.append(got - strided(nodes, own + my_first + i * my_tile, my_sub))
                for i in range(4):
                    two = jnp.concatenate(done[2 * i : 2 * i + 2], axis=0).astype(BF)
                    jump[slot, f * 64 + 16 * i : f * 64 + 16 * i + 16, h * 128 : h * 128 + 128] = two

        damp = [1.0 - 0.5 * smem_tabs[l, 2 * q + h, 12].astype(F32) for h in range(2)]
        for m in range(4):
            lifted = jnp.dot(
                lift_ref[m * 128 : m * 128 + 128, :], jump[slot], preferred_element_type=F32
            )
            for h in range(2):
                e = 2 * q + h
                here = nodes[at(((l + 1) * 8 + e) * NODES + m * 128, 128), :]
                sent[at((l * 8 + e) * NODES + m * 128, 128), :] = (
                    damp[h] * here + lifted[:, h * 128 : h * 128 + 128]
                ).astype(BF)

        @pl.when(s > 0)
        def _():
            send_step(s - 1)

    send_step(15)

    TN = (((0,), (0,)), ((), ()))

    def out_copy(q):
        rows = at(q * PAIR, PAIR)
        return pltpu.make_async_copy(whole.at[rows, :], out_ref.at[rows, :], out_sem.at[q])

    gram[...] = jnp.zeros_like(gram)

    @pl.loop(0, 4)
    def _(q):
        own_copy(q).wait()

        @pl.loop(1, 4)
        def _(o):
            src = lax.rem(t + o, 4)
            remote(
                sent.at[at(q * PAIR, PAIR), :],
                whole.at[at(q * PAIR, PAIR), at(src * 128, 128, 128)],
                send_sem.at[src, q], recv_sem.at[src, q], column(src),
            ).wait_recv()

        out_copy(q).start()
        rows = at(q * PAIR, PAIR)
        v = whole[rows, :]
        for b in range(2):
            left = v[:, b * 256 : b * 256 + 256]
            gram[b * 256 : b * 256 + 256, b * 256 : 512] += lax.dot_general(
                left, v[:, b * 256 : 512], TN, preferred_element_type=F32
            )

    scale = 1.0 / (1024 * NODES)
    index = 0
    for bi in range(4):
        for bj in range(bi, 4):
            part[index * 128 : index * 128 + 128, :] = (
                gram[bi * 128 : bi * 128 + 128, bj * 128 : bj * 128 + 128] * scale
            )
            index += 1

    HALF, PART = TILES // 2, TILES // 32
    keep, give = c * HALF, (1 - c) * HALF
    core = remote(part.at[at(give, HALF), :], core_in, core_send, core_recv, partner)
    core.start()
    core.wait_recv()
    part[at(keep, HALF), :] = part[at(keep, HALF), :] + core_in[...]

    def to_owner(o):
        p = lax.rem(xy + o, 16)
        return remote(
            part.at[at(keep + p * PART, PART), :], plane_in.at[xy], plane_send.at[p], plane_recv.at[xy], plane(xy + o)
        )

    def from_peer(o):
        p = lax.rem(xy + o, 16)
        return remote(
            part.at[at(keep, PART), :], plane_in.at[p], plane_send.at[p], plane_recv.at[p], plane(xy + o)
        )

    @pl.loop(1, 16)
    def _(o):
        to_owner(o).start()

    plane_in[xy] = part[at(keep + xy * PART, PART), :]

    @pl.loop(1, 16)
    def _(o):
        from_peer(o).wait_recv()

    total = plane_in[0]
    for p in range(1, 16):
        total = total + plane_in[p]
    z_in[t] = total

    def to_column(o):
        dst = lax.rem(t + o, 4)
        return remote(z_in.at[t], z_in.at[t], z_send.at[o - 1], z_recv.at[t], column(dst))

    for o in range(1, 4):
        to_column(o).start()
    for o in range(1, 4):
        src = lax.rem(t + o, 4)
        remote(z_in.at[src], z_in.at[src], z_send.at[o - 1], z_recv.at[src], column(src)).wait_recv()

    def own_rows(p):
        return gram_ref.at[at(keep + p * PART, PART), :]

    def back(o):
        return remote(own_rows(xy), own_rows(xy), back_send.at[o], back_recv.at[xy], plane(xy + o))

    def back_from(o):
        p = lax.rem(xy + o, 16)
        return remote(own_rows(p), own_rows(p), back_send.at[o], back_recv.at[p], plane(xy + o))

    def across_core(p):
        return remote(own_rows(p), own_rows(p), pair_send.at[p], pair_recv.at[p], partner)

    def across_core_in(p):
        rows = gram_ref.at[at(give + p * PART, PART), :]
        return remote(rows, rows, pair_send.at[p], pair_recv.at[p], partner)

    gram_ref[at(keep + xy * PART, PART), :] = (z_in[0] + z_in[1]) + (z_in[2] + z_in[3])

    @pl.loop(1, 16)
    def _(o):
        back(o).start()

    across_core(xy).start()

    @pl.loop(1, 16)
    def _(o):
        back_from(o).wait_recv()
        across_core(lax.rem(xy + o, 16)).start()

    @pl.loop(0, 16)
    def _(p):
        across_core_in(p).wait_recv()

    for o in range(1, 4):
        tab_copy(o).wait_send()
        to_column(o).wait_send()
    up.wait_send()
    down.wait_send()
    core.wait_send()

    @pl.loop(0, 16)
    def _(s):
        q, l = split_step(s)

        @pl.when(l != t)
        def _():
            layer_copy(q, l).wait_send()

    @pl.loop(1, 16)
    def _(o):
        to_owner(o).wait_send()
        back(o).wait_send()

    @pl.loop(0, 16)
    def _(p):
        across_core(p).wait_send()

    @pl.loop(0, 4)
    def _(q):
        out_copy(q).wait()


def weigh_and_gram(snapshots, lift, table):
    vm = pl.BlockSpec(memory_space=pltpu.VMEM)
    anyspace = pl.BlockSpec(memory_space=pl.ANY)
    D = pltpu.SemaphoreType.DMA
    V = pltpu.VMEM
    return pl.pallas_call(
        weigh_kernel,
        name="weigh_gram",
        out_shape=(jax.ShapeDtypeStruct((LAYER, 512), BF), jax.ShapeDtypeStruct((TILES, 128), F32)),
        in_specs=[anyspace, vm, vm],
        out_specs=(anyspace, vm),
        scratch_shapes=[
            V((4 * LAYER, 128), BF), V((6 * LAYER, 128), F32), V((4 * LAYER, 128), BF), V((LAYER, 512), BF),
            V((4, 8, 128), jnp.int32), pltpu.SMEM((4, 8, 128), jnp.int32),
            V((NODES, 128), BF), V((NODES, 128), BF), V((NODES, 128), BF), V((NODES, 128), BF),
            V((2, 384, 256), BF), V((512, 512), F32), V((TILES, 128), F32), V((TILES // 2, 128), F32),
            V((16, TILES // 32, 128), F32), V((4, TILES // 32, 128), F32),
            D((4,)), D((4,)), D((3,)), D((4,)), D(()), D((2,)), D((2,)),
            D((4, 4)), D((4, 4)), D((5,)), D(()), D(()), D((16,)), D((16,)),
            D((3,)), D((4,)), D((16,)), D((16,)), D((16,)), D((16,)),
        ],
        compiler_params=pltpu.CompilerParams(collective_id=0, has_side_effects=True),
    )(snapshots, lift, table)


def lanes_of(x, lane):
    return jnp.broadcast_to(x[:, lane : lane + 1], x.shape)


def row_of(x, row):
    return jnp.broadcast_to(x[row : row + 1, :], x.shape)


def factor_block(a, e):
    tiles = len(a)
    sub = lax.broadcasted_iota(jnp.int32, (8, 128), 0)
    upper, inverse = [], []
    for p in range(tiles):
        s = 8 * p
        c = [lanes_of(a[p], s + j) for j in range(8)]
        pa, pe = a[p], e[p]
        ra, re = pa, pe
        for j in range(8):
            d = row_of(c[j], j)
            inv = 1.0 / d
            scale = lax.rsqrt(d)
            here = sub == j
            m = jnp.where(here, -inv, c[j] * inv)
            qa, qe = row_of(pa, j), row_of(pe, j)
            ra = jnp.where(here, qa * scale, ra)
            re = jnp.where(here, qe * scale, re)
            pa = jnp.where(here, 0.0, pa) - m * qa
            pe = jnp.where(here, 0.0, pe) - m * qe
            for k in range(j + 1, 8):
                ck = row_of(c[k], j)
                c[k] = jnp.where(here, 0.0, c[k]) - m * ck
        upper.append(ra)
        inverse.append(re)
        qa = [row_of(pa, j) for j in range(8)]
        qe = [row_of(pe, j) for j in range(8)]
        for i in range(p + 1, tiles):
            l = [lanes_of(a[i], s + j) for j in range(8)]
            ua = [l[j] * qa[j] for j in range(8)]
            ue = [l[j] * qe[j] for j in range(8)]
            a[i] = a[i] - (((ua[0] + ua[1]) + (ua[2] + ua[3])) + ((ua[4] + ua[5]) + (ua[6] + ua[7])))
            e[i] = e[i] - (((ue[0] + ue[1]) + (ue[2] + ue[3])) + ((ue[4] + ue[5]) + (ue[6] + ue[7])))
    return upper, inverse


def chol_kernel(g_ref, w_ref, modes_ref, r_ref, work, inv_hi, inv_lo, stage, sem):
    n = r_ref.shape[0]
    blocks = n // 128
    rows = w_ref.shape[0]
    work[...] = jnp.zeros_like(work)
    index = 0
    for bi in range(blocks):
        for bj in range(bi, blocks):
            work[bi * 128 : bi * 128 + 128, bj * 128 : bj * 128 + 128] = g_ref[index * 128 : index * 128 + 128, :]
            index += 1
    sub = lax.broadcasted_iota(jnp.int32, (8, 128), 0)
    lane = lax.broadcasted_iota(jnp.int32, (8, 128), 1)

    def out_copy(kb):
        slot = lax.rem(kb, 2)
        return pltpu.make_async_copy(
            stage.at[slot], modes_ref.at[:, pl.ds(pl.multiple_of(kb * 128, 128), 128)], sem.at[slot]
        )

    @pl.loop(0, blocks)
    def _(kb):
        r0 = pl.multiple_of(kb * 128, 128)
        a = [work[pl.ds(pl.multiple_of(r0 + 8 * i, 8), 8), pl.ds(r0, 128)] for i in range(16)]
        e = [jnp.where(lane == sub + 8 * i, 1.0, 0.0) for i in range(16)]
        upper, inverse = factor_block(a, e)
        for i in range(16):
            work[pl.ds(pl.multiple_of(r0 + 8 * i, 8), 8), pl.ds(r0, 128)] = upper[i]
            work[pl.ds(pl.multiple_of(r0 + 8 * i, 8), 8), pl.ds(pl.multiple_of(r0 + n, 128), 128)] = inverse[i]
        own = pl.ds(r0, 128)
        linv = work[own, pl.ds(pl.multiple_of(r0 + n, 128), 128)]
        rest = pl.ds(pl.multiple_of(r0 + 128, 128), n - 128)
        work[own, rest] = jnp.dot(linv, work[own, rest], precision=HI, preferred_element_type=F32)

        @pl.loop(kb + 1, blocks)
        def _(i):
            ri = pl.multiple_of(i * 128, 128)
            left = work[own, pl.ds(ri, 128)].T
            window = pl.ds(pl.multiple_of(r0 + 128, 128), n)
            work[pl.ds(ri, 128), window] = work[pl.ds(ri, 128), window] - jnp.dot(
                left, work[own, window], precision=HI, preferred_element_type=F32
            )

        row = work[own, pl.ds(n, n)]
        hi = row.astype(BF)
        inv_hi[...] = hi
        inv_lo[...] = (row - hi.astype(F32)).astype(BF)

        @pl.when(kb >= 2)
        def _():
            out_copy(kb - 2).wait()

        slot = lax.rem(kb, 2)
        NT = (((1,), (1,)), ((), ()))

        @pl.loop(0, rows // 512)
        def _(q):
            part = pl.ds(pl.multiple_of(q * 512, 512), 512)
            x = w_ref[part, :]
            stage[slot, part, :] = lax.dot_general(
                x, inv_hi[...], NT, preferred_element_type=F32
            ) + lax.dot_general(x, inv_lo[...], NT, preferred_element_type=F32)

        out_copy(kb).start()

    out_copy(blocks - 2).wait()
    out_copy(blocks - 1).wait()
    ri = lax.broadcasted_iota(jnp.int32, (n, n), 0)
    ci = lax.broadcasted_iota(jnp.int32, (n, n), 1)
    r_ref[...] = jnp.where(ri <= ci, work[:, 0:n], 0.0)


def factor_and_modes(gram, weighted):
    rows, n = weighted.shape
    vm = pl.BlockSpec(memory_space=pltpu.VMEM)
    return pl.pallas_call(
        chol_kernel,
        name="factor_modes",
        out_shape=(jax.ShapeDtypeStruct((rows, n), F32), jax.ShapeDtypeStruct((n, n), F32)),
        in_specs=[vm, vm],
        out_specs=(pl.BlockSpec(memory_space=pl.ANY), vm),
        scratch_shapes=[
            pltpu.VMEM((n, 2 * n), F32),
            pltpu.VMEM((128, n), BF),
            pltpu.VMEM((128, n), BF),
            pltpu.VMEM((2, rows, 128), F32),
            pltpu.SemaphoreType.DMA((2,)),
        ],
    )(gram, weighted)


def on_device(snapshots, lift, adjacency, codes, obstacle):
    table = jnp.concatenate([adjacency, codes, obstacle[:, None]], axis=1)
    table = jnp.pad(table, ((0, 0), (0, 128 - table.shape[1])))
    weighted, gram = weigh_and_gram(snapshots, lift, table)
    return factor_and_modes(gram, weighted)


def solution(mesh):
    split = Mesh(
        mesh.devices.reshape(4, 4, 2, mesh.shape["tm"]), ("rows_0", "rows_1", "rows_2", "tm")
    )
    return jax.shard_map(
        on_device,
        mesh=split,
        in_specs=(P(ROWS, "tm"), P(), P(ROWS_TM, None), P(ROWS_TM, None), P(ROWS_TM)),
        out_specs=(P(ROWS_TM, None), P()),
        check_vma=False,
    )
```

```python
import jax
import jax.numpy as jnp
from jax import lax
from jax.experimental import pallas as pl
from jax.experimental.pallas import tpu as pltpu
from jax.sharding import Mesh
from jax.sharding import PartitionSpec as P

ROWS = ("rows_0", "rows_1", "rows_2")
ROWS_TM = ("rows_0", "rows_1", "rows_2", "tm")
HI = lax.Precision.HIGHEST
F32 = jnp.float32
BF = jnp.bfloat16
MESH = pl.DeviceIdType.MESH
NODES = 512
LAYER = 8 * NODES
PAIR = 2 * NODES
TILES = 1280


def at(start, size, step=8):
    return pl.ds(pl.multiple_of(start, step), size)


def halves(face):
    last = face % 2
    if face < 2:
        return last * 448, 8, 1
    if face < 4:
        return last * 56, 64, 1
    return last * 7, 64, 8


def strided(ref, start, step):
    return ref[pl.ds(start, 8), :] if step == 1 else ref[pl.ds(start, 8, stride=step), :]


def weigh_kernel(
    snap_ref, lift_ref, tab_ref, out_ref, gram_ref,
    raw, nodes, sent, whole, tabs, smem_tabs, up_face, down_face, low_halo, high_halo,
    jump, gram, part, core_in, plane_in, z_in,
    load_sem, out_sem, tab_send, tab_recv, smem_sem, halo_send, halo_recv,
    send_sem, recv_sem, own_sem, core_send, core_recv, plane_send, plane_recv,
    z_send, z_recv, back_send, back_recv, pair_send, pair_recv,
):
    y, x, c, t = (lax.axis_index(n) for n in ("rows_0", "rows_1", "rows_2", "tm"))
    r = (y * 4 + x) * 2 + c
    xy = y * 4 + x

    def group(index):
        index = lax.rem(index + 32, 32)
        return (index // 8, lax.rem(index // 2, 4), lax.rem(index, 2), t)

    def plane(index):
        index = lax.rem(index, 16)
        return (index // 4, lax.rem(index, 4), c, t)

    def column(index):
        return (y, x, c, index)

    partner = (y, x, 1 - c, t)
    other = (lambda: group(r + jnp.where(c == 1, 1, -1)))

    def remote(src, dst, send, recv, device):
        return pltpu.make_async_remote_copy(
            src_ref=src, dst_ref=dst, send_sem=send, recv_sem=recv, device_id=device, device_id_type=MESH
        )

    barrier = pltpu.get_barrier_semaphore()
    for o in range(1, 4):
        pl.semaphore_signal(barrier, inc=1, device_id=column(lax.rem(t + o, 4)), device_id_type=MESH)
    pl.semaphore_signal(barrier, inc=1, device_id=partner, device_id_type=MESH)
    pl.semaphore_signal(barrier, inc=1, device_id=other(), device_id_type=MESH)

    @pl.loop(1, 16)
    def _(o):
        pl.semaphore_signal(barrier, inc=1, device_id=plane(xy + o), device_id_type=MESH)

    def load(l):
        rows = at(l * LAYER, LAYER)
        return pltpu.make_async_copy(snap_ref.at[rows, :], raw.at[rows, :], load_sem.at[l])

    for l in (3, 0, 1, 2):
        load(l).start()
    for l in (3, 0, 1, 2):
        load(l).wait()

        @pl.loop(0, LAYER // 128)
        def _(i):
            nodes[at((l + 1) * LAYER + i * 128, 128), :] = raw[at(l * LAYER + i * 128, 128), :].astype(F32)

        if l in (3, 0):
            face, buffer = (7, up_face) if l == 3 else (0, down_face)

            @pl.loop(0, 32)
            def _(i):
                base = (l + 1) * LAYER + i * 128 + face
                two = [nodes[pl.ds(base + 64 * h, 8, stride=8), :] for h in range(2)]
                buffer[at(i * 16, 16, 16), :] = jnp.concatenate(two, axis=0).astype(BF)

    pl.semaphore_wait(barrier, 20)

    def tab_copy(o):
        return remote(tab_ref, tabs.at[t], tab_send.at[o - 1], tab_recv.at[t], column(lax.rem(t + o, 4)))

    for o in range(1, 4):
        tab_copy(o).start()
    up = remote(up_face, low_halo, halo_send.at[0], halo_recv.at[0], group(r + 1))
    down = remote(down_face, high_halo, halo_send.at[1], halo_recv.at[1], group(r - 1))
    up.start()
    down.start()
    mine = pltpu.make_async_copy(tab_ref, tabs.at[t], own_sem.at[4])
    mine.start()
    mine.wait()
    for o in range(1, 4):
        src = lax.rem(t + o, 4)
        remote(tab_ref, tabs.at[src], tab_send.at[o - 1], tab_recv.at[src], column(src)).wait_recv()
    to_smem = pltpu.make_async_copy(tabs, smem_tabs, smem_sem)
    to_smem.start()
    to_smem.wait()

    sub = lax.broadcasted_iota(jnp.int32, (8, 128), 0)

    def split_step(s):
        m = lax.rem(s, 4)
        return s // 4, jnp.where(m == 3, 3, lax.rem(m + 1, 3))

    def layer_copy(q, l):
        return remote(
            sent.at[at(l * LAYER + q * PAIR, PAIR), :],
            whole.at[at(q * PAIR, PAIR), at(t * 128, 128, 128)],
            send_sem.at[l, q], recv_sem.at[t, q], column(l),
        )

    def own_copy(q):
        return pltpu.make_async_copy(
            sent.at[at(t * LAYER + q * PAIR, PAIR), :],
            whole.at[at(q * PAIR, PAIR), at(t * 128, 128, 128)], own_sem.at[q],
        )

    def send_step(s):
        q, l = split_step(s)

        @pl.when(l == t)
        def _():
            own_copy(q).start()

        @pl.when(l != t)
        def _():
            layer_copy(q, l).start()

    @pl.loop(0, 16)
    def _(s):
        q, l = split_step(s)
        slot = lax.rem(s, 2)

        @pl.when(s == 2)
        def _():
            for copy, halo, layer, face in ((up, low_halo, 0, 7), (down, high_halo, 5, 0)):
                copy.wait_recv()

                @pl.loop(0, 32)
                def _(i):
                    two = halo[at(i * 16, 16, 16), :].astype(F32)
                    base = layer * LAYER + i * 128 + face
                    nodes[pl.ds(base, 8, stride=8), :] = two[0:8]
                    nodes[pl.ds(base + 64, 8, stride=8), :] = two[8:16]

        for h in range(2):
            e = 2 * q + h
            own = ((l + 1) * 8 + e) * NODES
            for f in range(6):
                n = smem_tabs[l, e, f]
                k = smem_tabs[l, e, 6 + f]
                shift = (0, 0, 0, 0, -1, 1)[f]
                base = ((l + 1 + shift) * 8 + (n & 7)) * NODES
                turn = jnp.where((k == 1) | (k == 2), 1, 0)
                odd = (k & 1) == 1
                order = jnp.where(k >= 2, 7 - sub, sub)
                wall = n < 0
                nb_first, nb_tile, nb_sub = halves(f ^ 1)
                my_first, my_tile, my_sub = halves(f)
                done = []
                for i in range(8):
                    j = i + turn * (7 - 2 * i)
                    straight = strided(nodes, base + nb_first + j * nb_tile, nb_sub)
                    across = strided(nodes, base + nb_first + j * nb_sub, nb_tile)
                    got = jnp.where(odd, across, straight)
                    got = jnp.take_along_axis(got, order, axis=0)
                    got = jnp.where(wall, 0.0, got)
                    done.append(got - strided(nodes, own + my_first + i * my_tile, my_sub))
                for i in range(4):
                    two = jnp.concatenate(done[2 * i : 2 * i + 2], axis=0).astype(BF)
                    jump[slot, f * 64 + 16 * i : f * 64 + 16 * i + 16, h * 128 : h * 128 + 128] = two

        damp = [1.0 - 0.5 * smem_tabs[l, 2 * q + h, 12].astype(F32) for h in range(2)]
        for m in range(4):
            lifted = jnp.dot(
                lift_ref[m * 128 : m * 128 + 128, :], jump[slot], preferred_element_type=F32
            )
            for h in range(2):
                e = 2 * q + h
                here = nodes[at(((l + 1) * 8 + e) * NODES + m * 128, 128), :]
                sent[at((l * 8 + e) * NODES + m * 128, 128), :] = (
                    damp[h] * here + lifted[:, h * 128 : h * 128 + 128]
                ).astype(BF)

        @pl.when(s > 0)
        def _():
            send_step(s - 1)

    send_step(15)

    TN = (((0,), (0,)), ((), ()))

    def out_copy(q):
        rows = at(q * PAIR, PAIR)
        return pltpu.make_async_copy(whole.at[rows, :], out_ref.at[rows, :], out_sem.at[q])

    gram[...] = jnp.zeros_like(gram)

    @pl.loop(0, 4)
    def _(q):
        own_copy(q).wait()

        @pl.loop(1, 4)
        def _(o):
            src = lax.rem(t + o, 4)
            remote(
                sent.at[at(q * PAIR, PAIR), :],
                whole.at[at(q * PAIR, PAIR), at(src * 128, 128, 128)],
                send_sem.at[src, q], recv_sem.at[src, q], column(src),
            ).wait_recv()

        out_copy(q).start()
        rows = at(q * PAIR, PAIR)
        v = whole[rows, :]
        for b in range(2):
            left = v[:, b * 256 : b * 256 + 256]
            gram[b * 256 : b * 256 + 256, b * 256 : 512] += lax.dot_general(
                left, v[:, b * 256 : 512], TN, preferred_element_type=F32
            )

    scale = 1.0 / (1024 * NODES)
    index = 0
    for bi in range(4):
        for bj in range(bi, 4):
            part[index * 128 : index * 128 + 128, :] = (
                gram[bi * 128 : bi * 128 + 128, bj * 128 : bj * 128 + 128] * scale
            )
            index += 1

    HALF, PART = TILES // 2, TILES // 32
    keep, give = c * HALF, (1 - c) * HALF
    core = remote(part.at[at(give, HALF), :], core_in, core_send, core_recv, partner)
    core.start()
    core.wait_recv()
    part[at(keep, HALF), :] = part[at(keep, HALF), :] + core_in[...]

    def to_owner(o):
        p = lax.rem(xy + o, 16)
        return remote(
            part.at[at(keep + p * PART, PART), :], plane_in.at[xy], plane_send.at[p], plane_recv.at[xy], plane(xy + o)
        )

    def from_peer(o):
        p = lax.rem(xy + o, 16)
        return remote(
            part.at[at(keep, PART), :], plane_in.at[p], plane_send.at[p], plane_recv.at[p], plane(xy + o)
        )

    @pl.loop(1, 16)
    def _(o):
        to_owner(o).start()

    plane_in[xy] = part[at(keep + xy * PART, PART), :]

    @pl.loop(1, 16)
    def _(o):
        from_peer(o).wait_recv()

    total = plane_in[0]
    for p in range(1, 16):
        total = total + plane_in[p]
    z_in[t] = total

    def to_column(o):
        dst = lax.rem(t + o, 4)
        return remote(z_in.at[t], z_in.at[t], z_send.at[o - 1], z_recv.at[t], column(dst))

    for o in range(1, 4):
        to_column(o).start()
    for o in range(1, 4):
        src = lax.rem(t + o, 4)
        remote(z_in.at[src], z_in.at[src], z_send.at[o - 1], z_recv.at[src], column(src)).wait_recv()

    def own_rows(p):
        return gram_ref.at[at(keep + p * PART, PART), :]

    def back(o):
        return remote(own_rows(xy), own_rows(xy), back_send.at[o], back_recv.at[xy], plane(xy + o))

    def back_from(o):
        p = lax.rem(xy + o, 16)
        return remote(own_rows(p), own_rows(p), back_send.at[o], back_recv.at[p], plane(xy + o))

    def across_core(p):
        return remote(own_rows(p), own_rows(p), pair_send.at[p], pair_recv.at[p], partner)

    def across_core_in(p):
        rows = gram_ref.at[at(give + p * PART, PART), :]
        return remote(rows, rows, pair_send.at[p], pair_recv.at[p], partner)

    gram_ref[at(keep + xy * PART, PART), :] = (z_in[0] + z_in[1]) + (z_in[2] + z_in[3])

    @pl.loop(1, 16)
    def _(o):
        back(o).start()

    across_core(xy).start()

    @pl.loop(1, 16)
    def _(o):
        back_from(o).wait_recv()
        across_core(lax.rem(xy + o, 16)).start()

    @pl.loop(0, 16)
    def _(p):
        across_core_in(p).wait_recv()

    for o in range(1, 4):
        tab_copy(o).wait_send()
        to_column(o).wait_send()
    up.wait_send()
    down.wait_send()
    core.wait_send()

    @pl.loop(0, 16)
    def _(s):
        q, l = split_step(s)

        @pl.when(l != t)
        def _():
            layer_copy(q, l).wait_send()

    @pl.loop(1, 16)
    def _(o):
        to_owner(o).wait_send()
        back(o).wait_send()

    @pl.loop(0, 16)
    def _(p):
        across_core(p).wait_send()

    @pl.loop(0, 4)
    def _(q):
        out_copy(q).wait()


def weigh_and_gram(snapshots, lift, table):
    vm = pl.BlockSpec(memory_space=pltpu.VMEM)
    anyspace = pl.BlockSpec(memory_space=pl.ANY)
    D = pltpu.SemaphoreType.DMA
    V = pltpu.VMEM
    return pl.pallas_call(
        weigh_kernel,
        name="weigh_gram",
        out_shape=(jax.ShapeDtypeStruct((LAYER, 512), BF), jax.ShapeDtypeStruct((TILES, 128), F32)),
        in_specs=[anyspace, vm, vm],
        out_specs=(anyspace, vm),
        scratch_shapes=[
            V((4 * LAYER, 128), BF), V((6 * LAYER, 128), F32), V((4 * LAYER, 128), BF), V((LAYER, 512), BF),
            V((4, 8, 128), jnp.int32), pltpu.SMEM((4, 8, 128), jnp.int32),
            V((NODES, 128), BF), V((NODES, 128), BF), V((NODES, 128), BF), V((NODES, 128), BF),
            V((2, 384, 256), BF), V((512, 512), F32), V((TILES, 128), F32), V((TILES // 2, 128), F32),
            V((16, TILES // 32, 128), F32), V((4, TILES // 32, 128), F32),
            D((4,)), D((4,)), D((3,)), D((4,)), D(()), D((2,)), D((2,)),
            D((4, 4)), D((4, 4)), D((5,)), D(()), D(()), D((16,)), D((16,)),
            D((3,)), D((4,)), D((16,)), D((16,)), D((16,)), D((16,)),
        ],
        compiler_params=pltpu.CompilerParams(collective_id=0, has_side_effects=True),
    )(snapshots, lift, table)


def lanes_of(x, lane):
    return jnp.broadcast_to(x[:, lane : lane + 1], x.shape)


def row_of(x, row):
    return jnp.broadcast_to(x[row : row + 1, :], x.shape)


def factor_block(a, e):
    tiles = len(a)
    sub = lax.broadcasted_iota(jnp.int32, (8, 128), 0)
    upper, inverse = [], []
    for p in range(tiles):
        s = 8 * p
        c = [lanes_of(a[p], s + j) for j in range(8)]
        pa, pe = a[p], e[p]
        ra, re = pa, pe
        for j in range(8):
            d = row_of(c[j], j)
            inv = 1.0 / d
            scale = lax.rsqrt(d)
            here = sub == j
            m = jnp.where(here, -inv, c[j] * inv)
            qa, qe = row_of(pa, j), row_of(pe, j)
            ra = jnp.where(here, qa * scale, ra)
            re = jnp.where(here, qe * scale, re)
            pa = jnp.where(here, 0.0, pa) - m * qa
            pe = jnp.where(here, 0.0, pe) - m * qe
            for k in range(j + 1, 8):
                ck = row_of(c[k], j)
                c[k] = jnp.where(here, 0.0, c[k]) - m * ck
        upper.append(ra)
        inverse.append(re)
        qa = [row_of(pa, j) for j in range(8)]
        qe = [row_of(pe, j) for j in range(8)]
        for i in range(p + 1, tiles):
            l = [lanes_of(a[i], s + j) for j in range(8)]
            ua = [l[j] * qa[j] for j in range(8)]
            ue = [l[j] * qe[j] for j in range(8)]
            a[i] = a[i] - (((ua[0] + ua[1]) + (ua[2] + ua[3])) + ((ua[4] + ua[5]) + (ua[6] + ua[7])))
            e[i] = e[i] - (((ue[0] + ue[1]) + (ue[2] + ue[3])) + ((ue[4] + ue[5]) + (ue[6] + ue[7])))
    return upper, inverse


def chol_kernel(g_ref, w_hbm, modes_ref, r_ref, work, w_ref, first, second, stage, sem, w_sem):
    n = r_ref.shape[0]
    blocks = n // 128
    rows = w_ref.shape[0]
    chunk = stage.shape[1]
    half = n // 2
    bring = pltpu.make_async_copy(w_hbm, w_ref, w_sem)
    bring.start()
    work[...] = jnp.zeros_like(work)
    index = 0
    for bi in range(blocks):
        for bj in range(bi, blocks):
            work[bi * 128 : bi * 128 + 128, bj * 128 : bj * 128 + 128] = g_ref[index * 128 : index * 128 + 128, :]
            index += 1
    sub = lax.broadcasted_iota(jnp.int32, (8, 128), 0)
    lane = lax.broadcasted_iota(jnp.int32, (8, 128), 1)

    @pl.loop(0, blocks)
    def _(kb):
        r0 = pl.multiple_of(kb * 128, 128)
        a = [work[pl.ds(pl.multiple_of(r0 + 8 * i, 8), 8), pl.ds(r0, 128)] for i in range(16)]
        e = [jnp.where(lane == sub + 8 * i, 1.0, 0.0) for i in range(16)]
        upper, inverse = factor_block(a, e)
        for i in range(16):
            work[pl.ds(pl.multiple_of(r0 + 8 * i, 8), 8), pl.ds(r0, 128)] = upper[i]
            work[pl.ds(pl.multiple_of(r0 + 8 * i, 8), 8), pl.ds(pl.multiple_of(r0 + n, 128), 128)] = inverse[i]
        own = pl.ds(r0, 128)
        linv = work[own, pl.ds(pl.multiple_of(r0 + n, 128), 128)]
        rest = pl.ds(pl.multiple_of(r0 + 128, 128), n - 128)
        work[own, rest] = jnp.dot(linv, work[own, rest], precision=HI, preferred_element_type=F32)

        @pl.loop(kb + 1, blocks)
        def _(i):
            ri = pl.multiple_of(i * 128, 128)
            left = work[own, pl.ds(ri, 128)].T
            window = pl.ds(pl.multiple_of(r0 + 128, 128), n)
            work[pl.ds(ri, 128), window] = work[pl.ds(ri, 128), window] - jnp.dot(
                left, work[own, window], precision=HI, preferred_element_type=F32
            )

    for part, r0, depth in ((first, 0, half), (second, half, n)):
        row = work[r0 : r0 + half, n : n + depth]
        high = row.astype(BF)
        part[:, 0:depth] = high
        part[:, depth : 2 * depth] = (row - high.astype(F32)).astype(BF)
    bring.wait()
    NT = (((1,), (1,)), ((), ()))

    def out_copy(q):
        slot = lax.rem(q, 2)
        return pltpu.make_async_copy(
            stage.at[slot], modes_ref.at[pl.ds(pl.multiple_of(q * chunk, chunk), chunk), :], sem.at[slot]
        )

    @pl.loop(0, rows // chunk)
    def _(q):
        slot = lax.rem(q, 2)

        @pl.when(q >= 2)
        def _():
            out_copy(q - 2).wait()

        x = w_ref[pl.ds(pl.multiple_of(q * chunk, chunk), chunk), :]
        near = x[:, 0:half]
        stage[slot, :, 0:half] = lax.dot_general(
            jnp.concatenate([near, near], axis=1), first[...], NT, preferred_element_type=F32
        )
        stage[slot, :, half:n] = lax.dot_general(
            jnp.concatenate([x, x], axis=1), second[...], NT, preferred_element_type=F32
        )
        out_copy(q).start()

    out_copy(rows // chunk - 2).wait()
    out_copy(rows // chunk - 1).wait()
    ri = lax.broadcasted_iota(jnp.int32, (n, n), 0)
    ci = lax.broadcasted_iota(jnp.int32, (n, n), 1)
    r_ref[...] = jnp.where(ri <= ci, work[:, 0:n], 0.0)


def factor_and_modes(gram, weighted):
    rows, n = weighted.shape
    vm = pl.BlockSpec(memory_space=pltpu.VMEM)
    anyspace = pl.BlockSpec(memory_space=pl.ANY)
    return pl.pallas_call(
        chol_kernel,
        name="factor_modes",
        out_shape=(jax.ShapeDtypeStruct((rows, n), F32), jax.ShapeDtypeStruct((n, n), F32)),
        in_specs=[vm, anyspace],
        out_specs=(anyspace, vm),
        scratch_shapes=[
            pltpu.VMEM((n, 2 * n), F32),
            pltpu.VMEM((rows, n), BF),
            pltpu.VMEM((n // 2, n), BF),
            pltpu.VMEM((n // 2, 2 * n), BF),
            pltpu.VMEM((2, 512, n), F32),
            pltpu.SemaphoreType.DMA((2,)),
            pltpu.SemaphoreType.DMA(()),
        ],
    )(gram, weighted)


def on_device(snapshots, lift, adjacency, codes, obstacle):
    table = jnp.concatenate([adjacency, codes, obstacle[:, None]], axis=1)
    table = jnp.pad(table, ((0, 0), (0, 128 - table.shape[1])))
    weighted, gram = weigh_and_gram(snapshots, lift, table)
    return factor_and_modes(gram, weighted)


def solution(mesh):
    split = Mesh(
        mesh.devices.reshape(4, 4, 2, mesh.shape["tm"]), ("rows_0", "rows_1", "rows_2", "tm")
    )
    return jax.shard_map(
        on_device,
        mesh=split,
        in_specs=(P(ROWS, "tm"), P(), P(ROWS_TM, None), P(ROWS_TM, None), P(ROWS_TM)),
        out_specs=(P(ROWS_TM, None), P()),
        check_vma=False,
    )
```

```python
import jax
import jax.numpy as jnp
from jax import lax
from jax.experimental import pallas as pl
from jax.experimental.pallas import tpu as pltpu
from jax.sharding import Mesh
from jax.sharding import PartitionSpec as P

ROWS = ("rows_0", "rows_1", "rows_2")
ROWS_TM = ("rows_0", "rows_1", "rows_2", "tm")
HI = lax.Precision.HIGHEST
F32 = jnp.float32
BF = jnp.bfloat16
MESH = pl.DeviceIdType.MESH
NODES = 512
LAYER = 8 * NODES
PAIR = 2 * NODES
TILES = 1280


def at(start, size, step=8):
    return pl.ds(pl.multiple_of(start, step), size)


def halves(face):
    last = face % 2
    if face < 2:
        return last * 448, 8, 1
    if face < 4:
        return last * 56, 64, 1
    return last * 7, 64, 8


def strided(ref, start, step):
    return ref[pl.ds(start, 8), :] if step == 1 else ref[pl.ds(start, 8, stride=step), :]


def weigh_kernel(
    snap_ref, lift_hbm, adjacency_ref, codes_ref, obstacle_ref, out_ref, gram_ref,
    lift_ref, lift_sem, raw, nodes, sent, whole, table, tabs, words, smem_words, up_face, down_face, low_halo, high_halo,
    jump, gram, part, core_in, plane_in, z_in,
    load_sem, out_sem, tab_send, tab_recv, smem_sem, halo_send, halo_recv,
    send_sem, recv_sem, own_sem, core_send, core_recv, plane_send, plane_recv,
    z_send, z_recv, back_send, back_recv, pair_send, pair_recv,
):
    y, x, c, t = (lax.axis_index(n) for n in ("rows_0", "rows_1", "rows_2", "tm"))
    r = (y * 4 + x) * 2 + c
    xy = y * 4 + x

    def group(index):
        index = lax.rem(index + 32, 32)
        return (index // 8, lax.rem(index // 2, 4), lax.rem(index, 2), t)

    def plane(index):
        index = lax.rem(index, 16)
        return (index // 4, lax.rem(index, 4), c, t)

    def column(index):
        return (y, x, c, index)

    partner = (y, x, 1 - c, t)

    def remote(src, dst, send, recv, device):
        return pltpu.make_async_remote_copy(
            src_ref=src, dst_ref=dst, send_sem=send, recv_sem=recv, device_id=device, device_id_type=MESH
        )

    barrier = pltpu.get_barrier_semaphore()

    @pl.loop(1, 16)
    def _(o):
        pl.semaphore_signal(barrier, inc=1, device_id=plane(xy + o), device_id_type=MESH)

    for o in range(1, 4):
        pl.semaphore_signal(barrier, inc=1, device_id=column(lax.rem(t + o, 4)), device_id_type=MESH)
    pl.semaphore_signal(barrier, inc=1, device_id=partner, device_id_type=MESH)
    pl.semaphore_signal(
        barrier, inc=1, device_id=group(r + jnp.where(c == 1, 1, -1)), device_id_type=MESH
    )

    def load(l):
        rows = at(l * LAYER, LAYER)
        return pltpu.make_async_copy(snap_ref.at[rows, :], raw.at[rows, :], load_sem.at[l])

    for l in (3, 0, 1, 2):
        load(l).start()
    bring_lift = pltpu.make_async_copy(lift_hbm, lift_ref, lift_sem)
    bring_lift.start()

    sub = lax.broadcasted_iota(jnp.int32, (8, 128), 0)
    blocked = jnp.zeros((8, 128), jnp.int32)
    for i in range(8):
        blocked = jnp.where(sub == i, obstacle_ref[i], blocked)
    table[...] = jnp.zeros_like(table)
    table[0, :, 0:6] = adjacency_ref[...]
    table[1, :, 0:6] = codes_ref[...]
    table[2] = blocked

    def widen(l):
        load(l).wait()

        @pl.loop(0, LAYER // 256)
        def _(i):
            nodes[at((l + 1) * LAYER + i * 256, 256), :] = raw[at(l * LAYER + i * 256, 256), :].astype(F32)

    def take_face(l, face, buffer):
        @pl.loop(0, 8)
        def _(i):
            for h in range(4):
                base = (l + 1) * LAYER + i * 512 + h * 128 + face
                two = [nodes[pl.ds(base + 64 * g, 8, stride=8), :] for g in range(2)]
                buffer[at(i * 64 + h * 16, 16, 16), :] = jnp.concatenate(two, axis=0).astype(BF)

    def tab_copy(o):
        return remote(table, tabs.at[t], tab_send.at[o - 1], tab_recv.at[t], column(lax.rem(t + o, 4)))

    up = remote(up_face, low_halo, halo_send.at[0], halo_recv.at[0], group(r + 1))
    down = remote(down_face, high_halo, halo_send.at[1], halo_recv.at[1], group(r - 1))
    mine = pltpu.make_async_copy(table, tabs.at[t], own_sem.at[8])
    mine.start()
    pl.semaphore_wait(barrier, 20)
    for o in (2, 1, 3):
        tab_copy(o).start()
    widen(3)
    take_face(3, 7, up_face)
    up.start()
    widen(0)
    take_face(0, 0, down_face)
    down.start()
    widen(1)
    widen(2)
    mine.wait()
    for o in range(1, 4):
        src = lax.rem(t + o, 4)
        remote(table, tabs.at[src], tab_send.at[o - 1], tab_recv.at[src], column(src)).wait_recv()
    lane = lax.broadcasted_iota(jnp.int32, (8, 128), 1)
    merged = jnp.zeros((8, 128), jnp.int32)
    for l in range(4):
        found, code, stop = tabs[l, 0], tabs[l, 1], tabs[l, 2]
        word = (found & 7) + 8 * code + jnp.where(found < 0, 32, 0) + 64 * stop
        merged = merged + pltpu.roll(jnp.where(lane < 6, word, 0), 8 * l, 1)
    words[...] = merged
    to_smem = pltpu.make_async_copy(words, smem_words, smem_sem)
    to_smem.start()
    to_smem.wait()

    def split_step(s):
        o = lax.rem(s, 3)
        odd = lax.rem(t, 2)
        other = jnp.where(o == 0, 1 + odd, jnp.where(o == 1, 3 * (1 - odd), lax.rem(t + 2, 4)))
        return jnp.where(s < 12, s // 3, s - 12), jnp.where(s < 12, other, t)

    def layer_copy(e, l):
        return remote(
            sent.at[at(l * LAYER + e * NODES, NODES), :],
            whole.at[at(e * NODES, NODES), at(t * 128, 128, 128)],
            send_sem.at[l, e], recv_sem.at[t, e], column(l),
        )

    def own_copy(e):
        return pltpu.make_async_copy(
            sent.at[at(t * LAYER + e * NODES, NODES), :],
            whole.at[at(e * NODES, NODES), at(t * 128, 128, 128)], own_sem.at[e],
        )

    def send_step(s):
        q, l = split_step(s)

        @pl.when(s >= 12)
        def _():
            for h in range(2):
                own_copy(2 * q + h).start()

        @pl.when(s < 12)
        def _():
            for h in range(2):
                layer_copy(2 * q + h, l).start()

    def jumps_of(s, slot):
        q, l = split_step(s)
        for h in range(2):
            e = 2 * q + h
            own = ((l + 1) * 8 + e) * NODES
            for f in range(6):
                word = smem_words[e, 8 * l + f]
                n = word & 7
                k = (word >> 3) & 3
                shift = (0, 0, 0, 0, -1, 1)[f]
                base = ((l + 1 + shift) * 8 + n) * NODES
                turn = jnp.where((k == 1) | (k == 2), 1, 0)
                odd = (k & 1) == 1
                order = jnp.where(k >= 2, 7 - sub, sub)
                wall = (word & 32) != 0
                nb_first, nb_tile, nb_sub = halves(f ^ 1)
                my_first, my_tile, my_sub = halves(f)
                done = []
                for i in range(8):
                    j = i + turn * (7 - 2 * i)
                    straight = strided(nodes, base + nb_first + j * nb_tile, nb_sub)
                    across = strided(nodes, base + nb_first + j * nb_sub, nb_tile)
                    got = jnp.where(odd, across, straight)
                    got = jnp.take_along_axis(got, order, axis=0)
                    got = jnp.where(wall, 0.0, got)
                    done.append(got - strided(nodes, own + my_first + i * my_tile, my_sub))
                for i in range(4):
                    two = jnp.concatenate(done[2 * i : 2 * i + 2], axis=0).astype(BF)
                    jump[slot, f * 64 + 16 * i : f * 64 + 16 * i + 16, h * 128 : h * 128 + 128] = two

    def weigh(s, slot):
        q, l = split_step(s)
        damp = [1.0 - 0.5 * (smem_words[2 * q + h, 8 * l] >> 6).astype(F32) for h in range(2)]
        for m in range(4):
            lifted = jnp.dot(
                lift_ref[m * 128 : m * 128 + 128, :], jump[slot], preferred_element_type=F32
            )
            for h in range(2):
                e = 2 * q + h
                here = nodes[at(((l + 1) * 8 + e) * NODES + m * 128, 128), :]
                sent[at((l * 8 + e) * NODES + m * 128, 128), :] = (
                    damp[h] * here + lifted[:, h * 128 : h * 128 + 128]
                ).astype(BF)

    jumps_of(0, 0)
    bring_lift.wait()
    for copy, halo, layer, face in ((up, low_halo, 0, 7), (down, high_halo, 5, 0)):
        copy.wait_recv()

        @pl.loop(0, 8)
        def _(i):
            for h in range(4):
                two = halo[at(i * 64 + h * 16, 16, 16), :].astype(F32)
                base = layer * LAYER + i * 512 + h * 128 + face
                nodes[pl.ds(base, 8, stride=8), :] = two[0:8]
                nodes[pl.ds(base + 64, 8, stride=8), :] = two[8:16]

    @pl.loop(0, 16)
    def _(s):
        slot = lax.rem(s, 2)
        weigh(s, slot)
        jumps_of(jnp.minimum(s + 1, 15), 1 - slot)
        send_step(s)

    TN = (((0,), (0,)), ((), ()))

    def out_copy(e):
        rows = at(e * NODES, NODES)
        return pltpu.make_async_copy(whole.at[rows, :], out_ref.at[rows, :], out_sem.at[e])

    gram[...] = jnp.zeros_like(gram)

    @pl.loop(0, 8)
    def _(e):
        own_copy(e).wait()

        @pl.loop(1, 4)
        def _(o):
            src = lax.rem(t + o, 4)
            remote(
                sent.at[at(e * NODES, NODES), :],
                whole.at[at(e * NODES, NODES), at(src * 128, 128, 128)],
                send_sem.at[src, e], recv_sem.at[src, e], column(src),
            ).wait_recv()

        out_copy(e).start()
        v = whole[at(e * NODES, NODES), :]
        for b in range(2):
            left = v[:, b * 256 : b * 256 + 256]
            gram[b * 256 : b * 256 + 256, b * 256 : 512] += lax.dot_general(
                left, v[:, b * 256 : 512], TN, preferred_element_type=F32
            )

    scale = 1.0 / (1024 * NODES)
    index = 0
    for bi in range(4):
        for bj in range(bi, 4):
            part[index * 128 : index * 128 + 128, :] = (
                gram[bi * 128 : bi * 128 + 128, bj * 128 : bj * 128 + 128] * scale
            )
            index += 1

    HALF, PART = TILES // 2, TILES // 32
    CHUNK = HALF // 4
    keep, give = c * HALF, (1 - c) * HALF

    def core(i):
        k = lax.rem(y + i, 4)
        rows = at(k * CHUNK, CHUNK)
        return remote(
            part.at[at(give + k * CHUNK, CHUNK), :], core_in.at[rows, :], core_send.at[k], core_recv.at[k], partner
        )

    def to_owner(p):
        return remote(
            part.at[at(keep + p * PART, PART), :], plane_in.at[xy], plane_send.at[p], plane_recv.at[xy], plane(p)
        )

    def from_peer(p):
        return remote(
            part.at[at(keep, PART), :], plane_in.at[p], plane_send.at[p], plane_recv.at[p], plane(p)
        )

    for i in range(4):
        core(i).start()

    for i in range(4):
        core(i).wait_recv()
        k = lax.rem(y + i, 4)
        mine_rows = at(keep + k * CHUNK, CHUNK)
        part[mine_rows, :] = part[mine_rows, :] + core_in[at(k * CHUNK, CHUNK), :]
        for o in range(1 if i == 0 else 0, 4):
            to_owner(k * 4 + lax.rem(x + o, 4)).start()

    plane_in[xy] = part[at(keep + xy * PART, PART), :]

    @pl.loop(1, 16)
    def _(o):
        from_peer(lax.rem(xy + o, 16)).wait_recv()

    total = plane_in[0]
    for p in range(1, 16):
        total = total + plane_in[p]
    z_in[t] = total

    def to_column(o):
        dst = lax.rem(t + o, 4)
        return remote(z_in.at[t], z_in.at[t], z_send.at[o - 1], z_recv.at[t], column(dst))

    for o in range(1, 4):
        to_column(o).start()
    for o in range(1, 4):
        src = lax.rem(t + o, 4)
        remote(z_in.at[src], z_in.at[src], z_send.at[o - 1], z_recv.at[src], column(src)).wait_recv()

    def own_rows(p):
        return gram_ref.at[at(keep + p * PART, PART), :]

    def back(o):
        return remote(own_rows(xy), own_rows(xy), back_send.at[o], back_recv.at[xy], plane(xy + o))

    def back_from(o):
        p = lax.rem(xy + o, 16)
        return remote(own_rows(p), own_rows(p), back_send.at[o], back_recv.at[p], plane(xy + o))

    def across_core(p):
        return remote(own_rows(p), own_rows(p), pair_send.at[p], pair_recv.at[p], partner)

    def across_core_in(p):
        rows = gram_ref.at[at(give + p * PART, PART), :]
        return remote(rows, rows, pair_send.at[p], pair_recv.at[p], partner)

    gram_ref[at(keep + xy * PART, PART), :] = (z_in[0] + z_in[1]) + (z_in[2] + z_in[3])

    @pl.loop(1, 16)
    def _(o):
        back(o).start()

    across_core(xy).start()

    @pl.loop(1, 16)
    def _(o):
        back_from(o).wait_recv()
        across_core(lax.rem(xy + o, 16)).start()

    @pl.loop(0, 16)
    def _(p):
        across_core_in(p).wait_recv()

    for o in range(1, 4):
        tab_copy(o).wait_send()
        to_column(o).wait_send()
    up.wait_send()
    down.wait_send()
    for i in range(4):
        core(i).wait_send()

    @pl.loop(0, 12)
    def _(s):
        q, l = split_step(s)
        for h in range(2):
            layer_copy(2 * q + h, l).wait_send()

    @pl.loop(1, 16)
    def _(o):
        to_owner(lax.rem(xy + o, 16)).wait_send()
        back(o).wait_send()

    @pl.loop(0, 16)
    def _(p):
        across_core(p).wait_send()

    @pl.loop(0, 8)
    def _(e):
        out_copy(e).wait()


def weigh_and_gram(snapshots, lift, adjacency, codes, obstacle):
    vm = pl.BlockSpec(memory_space=pltpu.VMEM)
    sm = pl.BlockSpec(memory_space=pltpu.SMEM)
    anyspace = pl.BlockSpec(memory_space=pl.ANY)
    D = pltpu.SemaphoreType.DMA
    V = pltpu.VMEM
    I32 = jnp.int32
    return pl.pallas_call(
        weigh_kernel,
        name="weigh_gram",
        out_shape=(jax.ShapeDtypeStruct((LAYER, 512), BF), jax.ShapeDtypeStruct((TILES, 128), F32)),
        in_specs=[anyspace, anyspace, vm, vm, sm],
        out_specs=(anyspace, vm),
        scratch_shapes=[
            V((NODES, 384), BF), D(()), V((4 * LAYER, 128), BF), V((6 * LAYER, 128), F32), V((4 * LAYER, 128), BF), V((LAYER, 512), BF),
            V((3, 8, 128), I32), V((4, 3, 8, 128), I32), V((8, 128), I32), pltpu.SMEM((8, 128), I32),
            V((NODES, 128), BF), V((NODES, 128), BF), V((NODES, 128), BF), V((NODES, 128), BF),
            V((2, 384, 256), BF), V((512, 512), F32), V((TILES, 128), F32), V((TILES // 2, 128), F32),
            V((16, TILES // 32, 128), F32), V((4, TILES // 32, 128), F32),
            D((4,)), D((8,)), D((3,)), D((4,)), D(()), D((2,)), D((2,)),
            D((4, 8)), D((4, 8)), D((9,)), D((4,)), D((4,)), D((16,)), D((16,)),
            D((3,)), D((4,)), D((16,)), D((16,)), D((16,)), D((16,)),
        ],
        compiler_params=pltpu.CompilerParams(collective_id=0, has_side_effects=True),
    )(snapshots, lift, adjacency, codes, obstacle)


NEAR = 2


def lanes_of(x, lane):
    return jnp.broadcast_to(x[:, lane : lane + 1], x.shape)


def row_of(x, row):
    return jnp.broadcast_to(x[row : row + 1, :], x.shape)


def factor_block(a):
    tiles = len(a)
    sub = lax.broadcasted_iota(jnp.int32, (8, 128), 0)
    lane = lax.broadcasted_iota(jnp.int32, (8, 128), 1)
    rows = []
    for p in range(tiles):
        s = 8 * p
        c = [lanes_of(a[p], s + j) for j in range(8)]
        pivot = a[p]
        row = pivot
        for j in range(8):
            d = row_of(c[j], j)
            inv = 1.0 / d
            scale = lax.rsqrt(d)
            here = sub == j
            m = jnp.where(here, -inv, c[j] * inv)
            pivot = jnp.where(lane == s + j, jnp.where(here, 1.0, 0.0), pivot)
            q = row_of(pivot, j)
            row = jnp.where(here, q * scale, row)
            pivot = jnp.where(here, 0.0, pivot) - m * q
            for k in range(j + 1, 8):
                ck = row_of(c[k], j)
                c[k] = jnp.where(here, 0.0, c[k]) - m * ck
        rows.append(row)
        q = [row_of(pivot, j) for j in range(8)]
        band = (lane >= s) & (lane < s + 8)
        far = p + 1 + NEAR
        if far < tiles:
            left = jnp.concatenate([a[i][:, s : s + 8] for i in range(far, tiles)], axis=0)
            prod = jnp.dot(left, pivot, precision=HI, preferred_element_type=F32)
        for i in range(p + 1, min(far, tiles)):
            u = [lanes_of(a[i], s + j) * q[j] for j in range(8)]
            a[i] = jnp.where(band, 0.0, a[i]) - (((u[0] + u[1]) + (u[2] + u[3])) + ((u[4] + u[5]) + (u[6] + u[7])))
        for i in range(far, tiles):
            at = 8 * (i - far)
            a[i] = jnp.where(band, 0.0, a[i]) - prod[at : at + 8, :]
    return rows


def chol_kernel(g_ref, w_hbm, modes_ref, r_ref, work, w_ref, first, second, stage, sem, w_sem):
    n = r_ref.shape[0]
    blocks = n // 128
    rows = w_ref.shape[0]
    chunk = stage.shape[1]
    half = n // 2
    bring = pltpu.make_async_copy(w_hbm, w_ref, w_sem)
    bring.start()
    work[...] = jnp.zeros_like(work)
    index = 0
    for bi in range(blocks):
        for bj in range(bi, blocks):
            work[bi * 128 : bi * 128 + 128, bj * 128 : bj * 128 + 128] = g_ref[index * 128 : index * 128 + 128, :]
            index += 1
    sub = lax.broadcasted_iota(jnp.int32, (8, 128), 0)
    lane = lax.broadcasted_iota(jnp.int32, (8, 128), 1)

    @pl.loop(0, blocks)
    def _(kb):
        r0 = pl.multiple_of(kb * 128, 128)
        a = [work[pl.ds(pl.multiple_of(r0 + 8 * i, 8), 8), pl.ds(r0, 128)] for i in range(16)]
        for i, row in enumerate(factor_block(a)):
            here = pl.ds(pl.multiple_of(r0 + 8 * i, 8), 8)
            diagonal, left = lane == sub + 8 * i, lane <= sub + 8 * i
            work[here, pl.ds(r0, 128)] = jnp.where(left, jnp.where(diagonal, 1.0 / row, 0.0), row)
            work[here, pl.ds(pl.multiple_of(r0 + n, 128), 128)] = jnp.where(left, row, 0.0)
        own = pl.ds(r0, 128)
        linv = work[own, pl.ds(pl.multiple_of(r0 + n, 128), 128)]
        rest = pl.ds(pl.multiple_of(r0 + 128, 128), n - 128)
        work[own, rest] = jnp.dot(linv, work[own, rest], precision=HI, preferred_element_type=F32)

        @pl.loop(kb + 1, blocks)
        def _(i):
            ri = pl.multiple_of(i * 128, 128)
            left = work[own, pl.ds(ri, 128)].T
            window = pl.ds(pl.multiple_of(r0 + 128, 128), n)
            work[pl.ds(ri, 128), window] = work[pl.ds(ri, 128), window] - jnp.dot(
                left, work[own, window], precision=HI, preferred_element_type=F32
            )

    for part, r0, depth in ((first, 0, half), (second, half, n)):
        row = work[r0 : r0 + half, n : n + depth]
        high = row.astype(BF)
        part[:, 0:depth] = high
        part[:, depth : 2 * depth] = (row - high.astype(F32)).astype(BF)
    bring.wait()
    NT = (((1,), (1,)), ((), ()))

    def out_copy(q):
        slot = lax.rem(q, 2)
        return pltpu.make_async_copy(
            stage.at[slot], modes_ref.at[pl.ds(pl.multiple_of(q * chunk, chunk), chunk), :], sem.at[slot]
        )

    @pl.loop(0, rows // chunk)
    def _(q):
        slot = lax.rem(q, 2)

        @pl.when(q >= 2)
        def _():
            out_copy(q - 2).wait()

        x = w_ref[pl.ds(pl.multiple_of(q * chunk, chunk), chunk), :]
        near = x[:, 0:half]
        stage[slot, :, 0:half] = lax.dot_general(
            jnp.concatenate([near, near], axis=1), first[...], NT, preferred_element_type=F32
        )
        stage[slot, :, half:n] = lax.dot_general(
            jnp.concatenate([x, x], axis=1), second[...], NT, preferred_element_type=F32
        )
        out_copy(q).start()

    out_copy(rows // chunk - 2).wait()
    out_copy(rows // chunk - 1).wait()
    ri = lax.broadcasted_iota(jnp.int32, (n, n), 0)
    ci = lax.broadcasted_iota(jnp.int32, (n, n), 1)
    r_ref[...] = jnp.where(ri <= ci, work[:, 0:n], 0.0)


def factor_and_modes(gram, weighted):
    rows, n = weighted.shape
    vm = pl.BlockSpec(memory_space=pltpu.VMEM)
    anyspace = pl.BlockSpec(memory_space=pl.ANY)
    return pl.pallas_call(
        chol_kernel,
        name="factor_modes",
        out_shape=(jax.ShapeDtypeStruct((rows, n), F32), jax.ShapeDtypeStruct((n, n), F32)),
        in_specs=[vm, anyspace],
        out_specs=(anyspace, vm),
        scratch_shapes=[
            pltpu.VMEM((n, 2 * n), F32),
            pltpu.VMEM((rows, n), BF),
            pltpu.VMEM((n // 2, n), BF),
            pltpu.VMEM((n // 2, 2 * n), BF),
            pltpu.VMEM((2, 512, n), F32),
            pltpu.SemaphoreType.DMA((2,)),
            pltpu.SemaphoreType.DMA(()),
        ],
    )(gram, weighted)


def on_device(snapshots, lift, adjacency, codes, obstacle):
    weighted, gram = weigh_and_gram(snapshots, lift, adjacency, codes, obstacle)
    return factor_and_modes(gram, weighted)


def solution(mesh):
    split = Mesh(
        mesh.devices.reshape(4, 4, 2, mesh.shape["tm"]), ("rows_0", "rows_1", "rows_2", "tm")
    )
    return jax.shard_map(
        on_device,
        mesh=split,
        in_specs=(P(ROWS, "tm"), P(), P(ROWS_TM, None), P(ROWS_TM, None), P(ROWS_TM)),
        out_specs=(P(ROWS_TM, None), P()),
        check_vma=False,
    )
```

```python
import functools

import jax
import jax.numpy as jnp
from jax import lax
from jax.experimental import pallas as pl
from jax.experimental.pallas import tpu as pltpu
from jax.sharding import Mesh
from jax.sharding import PartitionSpec as P

ROWS = ("rows_0", "rows_1", "rows_2")
ROWS_TM = ("rows_0", "rows_1", "rows_2", "tm")
HI = lax.Precision.HIGHEST
F32 = jnp.float32
BF = jnp.bfloat16
MESH = pl.DeviceIdType.MESH
NODES = 512
LAYER = 8 * NODES
PAIR = 2 * NODES
TILES = 1280


def at(start, size, step=8):
    return pl.ds(pl.multiple_of(start, step), size)


def halves(face):
    last = face % 2
    if face < 2:
        return last * 448, 8, 1
    if face < 4:
        return last * 56, 64, 1
    return last * 7, 64, 8


def strided(ref, start, step):
    return ref[pl.ds(start, 8), :] if step == 1 else ref[pl.ds(start, 8, stride=step), :]


def weigh_kernel(
    snap_ref, lift_hbm, adjacency_ref, codes_ref, obstacle_ref, out_ref, gram_ref,
    lift_ref, lift_sem, raw, nodes, sent, whole, table, tabs, words, smem_words, up_face, down_face, low_halo, high_halo,
    jump, gram, part, core_in, plane_in, z_in,
    load_sem, out_sem, tab_send, tab_recv, smem_sem, halo_send, halo_recv,
    send_sem, recv_sem, own_sem, core_send, core_recv, plane_send, plane_recv,
    z_send, z_recv, back_send, back_recv, pair_send, pair_recv,
):
    y, x, c, t = (lax.axis_index(n) for n in ("rows_0", "rows_1", "rows_2", "tm"))
    r = (y * 4 + x) * 2 + c
    xy = y * 4 + x

    def group(index):
        index = lax.rem(index + 32, 32)
        return (index // 8, lax.rem(index // 2, 4), lax.rem(index, 2), t)

    def plane(index):
        index = lax.rem(index, 16)
        return (index // 4, lax.rem(index, 4), c, t)

    def column(index):
        return (y, x, c, index)

    partner = (y, x, 1 - c, t)

    def remote(src, dst, send, recv, device):
        return pltpu.make_async_remote_copy(
            src_ref=src, dst_ref=dst, send_sem=send, recv_sem=recv, device_id=device, device_id_type=MESH
        )

    barrier = pltpu.get_barrier_semaphore()

    @pl.loop(1, 16)
    def _(o):
        pl.semaphore_signal(barrier, inc=1, device_id=plane(xy + o), device_id_type=MESH)

    for o in range(1, 4):
        pl.semaphore_signal(barrier, inc=1, device_id=column(lax.rem(t + o, 4)), device_id_type=MESH)
    pl.semaphore_signal(barrier, inc=1, device_id=partner, device_id_type=MESH)
    pl.semaphore_signal(
        barrier, inc=1, device_id=group(r + jnp.where(c == 1, 1, -1)), device_id_type=MESH
    )

    def load(l):
        rows = at(l * LAYER, LAYER)
        return pltpu.make_async_copy(snap_ref.at[rows, :], raw.at[rows, :], load_sem.at[l])

    for l in (3, 0, 1, 2):
        load(l).start()
    bring_lift = pltpu.make_async_copy(lift_hbm, lift_ref, lift_sem)
    bring_lift.start()

    sub = lax.broadcasted_iota(jnp.int32, (8, 128), 0)
    blocked = jnp.zeros((8, 128), jnp.int32)
    for i in range(8):
        blocked = jnp.where(sub == i, obstacle_ref[i], blocked)
    table[...] = jnp.zeros_like(table)
    table[0, :, 0:6] = adjacency_ref[...]
    table[1, :, 0:6] = codes_ref[...]
    table[2] = blocked

    def widen(l):
        load(l).wait()

        @pl.loop(0, LAYER // 256)
        def _(i):
            nodes[at((l + 1) * LAYER + i * 256, 256), :] = raw[at(l * LAYER + i * 256, 256), :].astype(F32)

    def take_face(l, face, buffer):
        @pl.loop(0, 8)
        def _(i):
            for h in range(4):
                base = (l + 1) * LAYER + i * 512 + h * 128 + face
                two = [nodes[pl.ds(base + 64 * g, 8, stride=8), :] for g in range(2)]
                buffer[at(i * 64 + h * 16, 16, 16), :] = jnp.concatenate(two, axis=0).astype(BF)

    def tab_copy(o):
        return remote(table, tabs.at[t], tab_send.at[o - 1], tab_recv.at[t], column(lax.rem(t + o, 4)))

    up = remote(up_face, low_halo, halo_send.at[0], halo_recv.at[0], group(r + 1))
    down = remote(down_face, high_halo, halo_send.at[1], halo_recv.at[1], group(r - 1))
    mine = pltpu.make_async_copy(table, tabs.at[t], own_sem.at[8])
    mine.start()
    pl.semaphore_wait(barrier, 20)
    for o in (2, 1, 3):
        tab_copy(o).start()
    widen(3)
    take_face(3, 7, up_face)
    up.start()
    widen(0)
    take_face(0, 0, down_face)
    down.start()
    widen(1)
    widen(2)
    mine.wait()
    for o in range(1, 4):
        src = lax.rem(t + o, 4)
        remote(table, tabs.at[src], tab_send.at[o - 1], tab_recv.at[src], column(src)).wait_recv()
    lane = lax.broadcasted_iota(jnp.int32, (8, 128), 1)
    merged = jnp.zeros((8, 128), jnp.int32)
    for l in range(4):
        found, code, stop = tabs[l, 0], tabs[l, 1], tabs[l, 2]
        word = (found & 7) + 8 * code + jnp.where(found < 0, 32, 0) + 64 * stop
        merged = merged + pltpu.roll(jnp.where(lane < 6, word, 0), 8 * l, 1)
    words[...] = merged
    to_smem = pltpu.make_async_copy(words, smem_words, smem_sem)
    to_smem.start()
    to_smem.wait()

    def split_step(s):
        o = lax.rem(s, 3)
        odd = lax.rem(t, 2)
        other = jnp.where(o == 0, 1 + odd, jnp.where(o == 1, 3 * (1 - odd), lax.rem(t + 2, 4)))
        return jnp.where(s < 12, s // 3, s - 12), jnp.where(s < 12, other, t)

    def layer_copy(e, l):
        return remote(
            sent.at[at(l * LAYER + e * NODES, NODES), :],
            whole.at[at(e * NODES, NODES), at(t * 128, 128, 128)],
            send_sem.at[l, e], recv_sem.at[t, e], column(l),
        )

    def own_copy(e):
        return pltpu.make_async_copy(
            sent.at[at(t * LAYER + e * NODES, NODES), :],
            whole.at[at(e * NODES, NODES), at(t * 128, 128, 128)], own_sem.at[e],
        )

    def send_step(s):
        q, l = split_step(s)

        @pl.when(s >= 12)
        def _():
            for h in range(2):
                own_copy(2 * q + h).start()

        @pl.when(s < 12)
        def _():
            for h in range(2):
                layer_copy(2 * q + h, l).start()

    def jumps_of(s, slot):
        q, l = split_step(s)
        for h in range(2):
            e = 2 * q + h
            own = ((l + 1) * 8 + e) * NODES
            for f in range(6):
                word = smem_words[e, 8 * l + f]
                n = word & 7
                k = (word >> 3) & 3
                shift = (0, 0, 0, 0, -1, 1)[f]
                base = ((l + 1 + shift) * 8 + n) * NODES
                turn = jnp.where((k == 1) | (k == 2), 1, 0)
                odd = (k & 1) == 1
                order = jnp.where(k >= 2, 7 - sub, sub)
                wall = (word & 32) != 0
                nb_first, nb_tile, nb_sub = halves(f ^ 1)
                my_first, my_tile, my_sub = halves(f)
                done = []
                for i in range(8):
                    j = i + turn * (7 - 2 * i)
                    straight = strided(nodes, base + nb_first + j * nb_tile, nb_sub)
                    across = strided(nodes, base + nb_first + j * nb_sub, nb_tile)
                    got = jnp.where(odd, across, straight)
                    got = jnp.take_along_axis(got, order, axis=0)
                    got = jnp.where(wall, 0.0, got)
                    done.append(got - strided(nodes, own + my_first + i * my_tile, my_sub))
                for i in range(4):
                    two = jnp.concatenate(done[2 * i : 2 * i + 2], axis=0).astype(BF)
                    jump[slot, f * 64 + 16 * i : f * 64 + 16 * i + 16, h * 128 : h * 128 + 128] = two

    def weigh(s, slot):
        q, l = split_step(s)
        damp = [1.0 - 0.5 * (smem_words[2 * q + h, 8 * l] >> 6).astype(F32) for h in range(2)]
        for m in range(4):
            lifted = jnp.dot(
                lift_ref[m * 128 : m * 128 + 128, :], jump[slot], preferred_element_type=F32
            )
            for h in range(2):
                e = 2 * q + h
                here = nodes[at(((l + 1) * 8 + e) * NODES + m * 128, 128), :]
                sent[at((l * 8 + e) * NODES + m * 128, 128), :] = (
                    damp[h] * here + lifted[:, h * 128 : h * 128 + 128]
                ).astype(BF)

    jumps_of(0, 0)
    bring_lift.wait()
    for copy, halo, layer, face in ((up, low_halo, 0, 7), (down, high_halo, 5, 0)):
        copy.wait_recv()

        @pl.loop(0, 8)
        def _(i):
            for h in range(4):
                two = halo[at(i * 64 + h * 16, 16, 16), :].astype(F32)
                base = layer * LAYER + i * 512 + h * 128 + face
                nodes[pl.ds(base, 8, stride=8), :] = two[0:8]
                nodes[pl.ds(base + 64, 8, stride=8), :] = two[8:16]

    @pl.loop(0, 16)
    def _(s):
        slot = lax.rem(s, 2)
        weigh(s, slot)
        jumps_of(jnp.minimum(s + 1, 15), 1 - slot)
        send_step(s)

    TN = (((0,), (0,)), ((), ()))

    def out_copy(e):
        rows = at(e * NODES, NODES)
        return pltpu.make_async_copy(whole.at[rows, :], out_ref.at[rows, :], out_sem.at[e])

    gram[...] = jnp.zeros_like(gram)

    @pl.loop(0, 8)
    def _(e):
        own_copy(e).wait()

        @pl.loop(1, 4)
        def _(o):
            src = lax.rem(t + o, 4)
            remote(
                sent.at[at(e * NODES, NODES), :],
                whole.at[at(e * NODES, NODES), at(src * 128, 128, 128)],
                send_sem.at[src, e], recv_sem.at[src, e], column(src),
            ).wait_recv()

        out_copy(e).start()
        v = whole[at(e * NODES, NODES), :]
        for b in range(2):
            left = v[:, b * 256 : b * 256 + 256]
            gram[b * 256 : b * 256 + 256, b * 256 : 512] += lax.dot_general(
                left, v[:, b * 256 : 512], TN, preferred_element_type=F32
            )

    scale = 1.0 / (1024 * NODES)
    index = 0
    for bi in range(4):
        for bj in range(bi, 4):
            part[index * 128 : index * 128 + 128, :] = (
                gram[bi * 128 : bi * 128 + 128, bj * 128 : bj * 128 + 128] * scale
            )
            index += 1

    HALF, PART = TILES // 2, TILES // 32
    CHUNK = HALF // 4
    keep, give = c * HALF, (1 - c) * HALF

    def core(i):
        k = lax.rem(y + i, 4)
        rows = at(k * CHUNK, CHUNK)
        return remote(
            part.at[at(give + k * CHUNK, CHUNK), :], core_in.at[rows, :], core_send.at[k], core_recv.at[k], partner
        )

    def to_owner(p):
        return remote(
            part.at[at(keep + p * PART, PART), :], plane_in.at[xy], plane_send.at[p], plane_recv.at[xy], plane(p)
        )

    def from_peer(p):
        return remote(
            part.at[at(keep, PART), :], plane_in.at[p], plane_send.at[p], plane_recv.at[p], plane(p)
        )

    for i in range(4):
        core(i).start()

    for i in range(4):
        core(i).wait_recv()
        k = lax.rem(y + i, 4)
        mine_rows = at(keep + k * CHUNK, CHUNK)
        part[mine_rows, :] = part[mine_rows, :] + core_in[at(k * CHUNK, CHUNK), :]
        for o in range(1 if i == 0 else 0, 4):
            to_owner(k * 4 + lax.rem(x + o, 4)).start()

    plane_in[xy] = part[at(keep + xy * PART, PART), :]

    @pl.loop(1, 16)
    def _(o):
        from_peer(lax.rem(xy + o, 16)).wait_recv()

    total = plane_in[0]
    for p in range(1, 16):
        total = total + plane_in[p]
    z_in[t] = total

    def to_column(o):
        dst = lax.rem(t + o, 4)
        return remote(z_in.at[t], z_in.at[t], z_send.at[o - 1], z_recv.at[t], column(dst))

    for o in range(1, 4):
        to_column(o).start()
    for o in range(1, 4):
        src = lax.rem(t + o, 4)
        remote(z_in.at[src], z_in.at[src], z_send.at[o - 1], z_recv.at[src], column(src)).wait_recv()

    def own_rows(p):
        return gram_ref.at[at(keep + p * PART, PART), :]

    def back(o):
        return remote(own_rows(xy), own_rows(xy), back_send.at[o], back_recv.at[xy], plane(xy + o))

    def back_from(o):
        p = lax.rem(xy + o, 16)
        return remote(own_rows(p), own_rows(p), back_send.at[o], back_recv.at[p], plane(xy + o))

    def across_core(p):
        return remote(own_rows(p), own_rows(p), pair_send.at[p], pair_recv.at[p], partner)

    def across_core_in(p):
        rows = gram_ref.at[at(give + p * PART, PART), :]
        return remote(rows, rows, pair_send.at[p], pair_recv.at[p], partner)

    gram_ref[at(keep + xy * PART, PART), :] = (z_in[0] + z_in[1]) + (z_in[2] + z_in[3])

    @pl.loop(1, 16)
    def _(o):
        back(o).start()

    across_core(xy).start()

    @pl.loop(1, 16)
    def _(o):
        back_from(o).wait_recv()
        across_core(lax.rem(xy + o, 16)).start()

    @pl.loop(0, 16)
    def _(p):
        across_core_in(p).wait_recv()

    for o in range(1, 4):
        tab_copy(o).wait_send()
        to_column(o).wait_send()
    up.wait_send()
    down.wait_send()
    for i in range(4):
        core(i).wait_send()

    @pl.loop(0, 12)
    def _(s):
        q, l = split_step(s)
        for h in range(2):
            layer_copy(2 * q + h, l).wait_send()

    @pl.loop(1, 16)
    def _(o):
        to_owner(lax.rem(xy + o, 16)).wait_send()
        back(o).wait_send()

    @pl.loop(0, 16)
    def _(p):
        across_core(p).wait_send()

    @pl.loop(0, 8)
    def _(e):
        out_copy(e).wait()


def weigh_and_gram(snapshots, lift, adjacency, codes, obstacle):
    vm = pl.BlockSpec(memory_space=pltpu.VMEM)
    sm = pl.BlockSpec(memory_space=pltpu.SMEM)
    anyspace = pl.BlockSpec(memory_space=pl.ANY)
    D = pltpu.SemaphoreType.DMA
    V = pltpu.VMEM
    I32 = jnp.int32
    return pl.pallas_call(
        weigh_kernel,
        name="weigh_gram",
        out_shape=(jax.ShapeDtypeStruct((LAYER, 512), BF), jax.ShapeDtypeStruct((TILES, 128), F32)),
        in_specs=[anyspace, anyspace, vm, vm, sm],
        out_specs=(anyspace, vm),
        scratch_shapes=[
            V((NODES, 384), BF), D(()), V((4 * LAYER, 128), BF), V((6 * LAYER, 128), F32), V((4 * LAYER, 128), BF), V((LAYER, 512), BF),
            V((3, 8, 128), I32), V((4, 3, 8, 128), I32), V((8, 128), I32), pltpu.SMEM((8, 128), I32),
            V((NODES, 128), BF), V((NODES, 128), BF), V((NODES, 128), BF), V((NODES, 128), BF),
            V((2, 384, 256), BF), V((512, 512), F32), V((TILES, 128), F32), V((TILES // 2, 128), F32),
            V((16, TILES // 32, 128), F32), V((4, TILES // 32, 128), F32),
            D((4,)), D((8,)), D((3,)), D((4,)), D(()), D((2,)), D((2,)),
            D((4, 8)), D((4, 8)), D((9,)), D((4,)), D((4,)), D((16,)), D((16,)),
            D((3,)), D((4,)), D((16,)), D((16,)), D((16,)), D((16,)),
        ],
        compiler_params=pltpu.CompilerParams(collective_id=0, has_side_effects=True),
    )(snapshots, lift, adjacency, codes, obstacle)


NEAR = 2


def lanes_of(x, lane):
    return jnp.broadcast_to(x[:, lane : lane + 1], x.shape)


def row_of(x, row):
    return jnp.broadcast_to(x[row : row + 1, :], x.shape)


def tree_sum(terms):
    while len(terms) > 1:
        terms = [terms[i] + terms[i + 1] for i in range(0, len(terms), 2)]
    return terms[0]


def eliminate(c, pivot, s, follow=None):
    sub = lax.broadcasted_iota(jnp.int32, (8, 128), 0)
    lane = lax.broadcasted_iota(jnp.int32, (8, 128), 1)
    row = pivot
    if follow:
        l, c2, nxt = follow
    for j in range(8):
        d = row_of(c[j], j)
        inv = 1.0 / d
        scale = lax.rsqrt(d)
        here, unit = sub == j, lane == s + j
        m = jnp.where(here, -inv, c[j] * inv)
        pivot = jnp.where(unit, jnp.where(here, 1.0, 0.0), pivot)
        q = row_of(pivot, j)
        row = jnp.where(here, q * scale, row)
        pivot = jnp.where(here, 0.0, pivot) - m * q
        heads = {k: row_of(c[k], j) for k in range(j + 1, 8)}
        for k in range(j + 1, 8):
            c[k] = jnp.where(here, 0.0, c[k]) - m * heads[k]
        if follow:
            ml = l[j] * inv
            nxt = jnp.where(unit, 0.0, nxt) - ml * q
            for k in range(8):
                c2[k] = c2[k] - ml * row_of(l[j], k)
            for k in range(j + 1, 8):
                l[k] = l[k] - ml * heads[k]
    return pivot, row, nxt if follow else None


def factor_block(a, beside):
    tiles = len(a)
    lane = lax.broadcasted_iota(jnp.int32, (8, 128), 1)
    rows = []
    for p in range(0, tiles, 2):
        s = 8 * p
        c = [lanes_of(a[p], s + j) for j in range(8)]
        l = [lanes_of(a[p + 1], s + j) for j in range(8)]
        c2 = [lanes_of(a[p + 1], s + 8 + j) for j in range(8)]
        far = p + 2 + NEAR
        near = range(p + 2, min(far, tiles))
        old = {i: [lanes_of(a[i], s + j) for j in range(16)] for i in near}
        q1, row, nxt = eliminate(c, a[p], s, (l, c2, a[p + 1]))
        rows.append(row)
        beside(p)
        u = [lanes_of(q1, s + 8 + j) for j in range(8)]
        q2, row, _ = eliminate(c2, nxt, s + 8)
        rows.append(row)
        beside(p + 1)
        if p + 2 == tiles:
            break
        heads = [row_of(q2, j) for j in range(8)]
        q1 = jnp.where((lane >= s + 8) & (lane < s + 16), 0.0, q1) - tree_sum([u[j] * heads[j] for j in range(8)])
        band = (lane >= s) & (lane < s + 16)
        if far < tiles:
            left = jnp.concatenate([a[i][:, s : s + 16] for i in range(far, tiles)], axis=0)
            prod = jnp.dot(left, jnp.concatenate([q1, q2], axis=0), precision=HI, preferred_element_type=F32)
        heads = [row_of(q1, j) for j in range(8)] + heads
        for i in near:
            a[i] = jnp.where(band, 0.0, a[i]) - tree_sum([old[i][j] * heads[j] for j in range(16)])
        for i in range(far, tiles):
            at = 8 * (i - far)
            a[i] = jnp.where(band, 0.0, a[i]) - prod[at : at + 8, :]
    return rows


def chol_kernel(g_ref, w_hbm, modes_ref, r_ref, work, w_ref, inv, stage, r_rows, sem, w_sem, r_sem, last_sem):
    n = r_ref.shape[1]
    blocks = n // 128
    rows = w_ref.shape[0]
    piece = rows // 16
    bring = pltpu.make_async_copy(w_hbm, w_ref, w_sem)
    bring.start()
    sub = lax.broadcasted_iota(jnp.int32, (8, 128), 0)
    lane = lax.broadcasted_iota(jnp.int32, (8, 128), 1)
    NT = (((1,), (1,)), ((), ()))
    order = [(i, j) for i in range(blocks) for j in range(i, blocks)]

    def cols(j, count=1):
        return pl.ds(j * 128, count * 128)

    for index, (i, j) in enumerate(order):
        work[cols(i), cols(j)] = g_ref[cols(index), :]
    for i in range(1, blocks):
        work[cols(i), cols(blocks, i)] = jnp.zeros((128, i * 128), F32)

    def update(kb, i):
        window = pl.ds(i * 128, n + (kb + 1 - i) * 128)
        left = work[cols(kb), cols(i)].T
        work[cols(i), window] = work[cols(i), window] - jnp.dot(
            left, work[cols(kb), window], precision=HI, preferred_element_type=F32
        )

    def product(kb, first, count):
        depth = (kb + 1) * 128
        x = w_ref[pl.ds(first, count), 0:depth]
        both = lax.dot_general(x, inv[kb % 2, :, 0:depth], NT, preferred_element_type=F32)
        stage[kb % 2, pl.ds(first, count), :] = both[:, 0:128] + both[:, 128:256]

    def out_copy(kb):
        return pltpu.make_async_copy(stage.at[kb % 2], modes_ref.at[:, cols(kb)], sem.at[kb % 2])

    def r_copy(kb):
        return pltpu.make_async_copy(r_rows.at[cols(kb), :], r_ref.at[cols(kb), :], r_sem.at[kb])

    for kb in range(blocks):
        waiting = []
        if kb >= 1:
            waiting = [functools.partial(update, kb - 1, i) for i in range(kb + 1, blocks)]

        def beside(p):
            if waiting:
                waiting.pop(0)()
            if kb >= 1:
                product(kb - 1, p * piece, piece)

        if kb == 1:
            bring.wait()
        if kb >= 3:
            out_copy(kb - 3).wait()
        a = [work[pl.ds(kb * 128 + 8 * i, 8), cols(kb)] for i in range(16)]
        for i, row in enumerate(factor_block(a, beside)):
            here = pl.ds(kb * 128 + 8 * i, 8)
            diagonal, left = lane == sub + 8 * i, lane <= sub + 8 * i
            r_rows[here, cols(kb)] = jnp.where(left, jnp.where(diagonal, 1.0 / row, 0.0), row)
            work[here, cols(kb + blocks)] = jnp.where(left, row, 0.0)
        if kb >= 1:
            out_copy(kb - 1).start()
        rest = pl.ds((kb + 1) * 128, n - 128)
        work[cols(kb), rest] = jnp.dot(
            work[cols(kb), cols(kb + blocks)], work[cols(kb), rest], precision=HI, preferred_element_type=F32
        )
        if kb + 1 < blocks:
            update(kb, kb + 1)
        depth = (kb + 1) * 128
        row = work[cols(kb), pl.ds(n, depth)]
        high = row.astype(BF)
        inv[kb % 2, 0:128, 0:depth] = high
        inv[kb % 2, 128:256, 0:depth] = (row - high.astype(F32)).astype(BF)
        if kb > 0:
            r_rows[cols(kb), cols(0, kb)] = jnp.zeros((128, kb * 128), F32)
        if kb + 1 < blocks:
            r_rows[cols(kb), cols(kb + 1, blocks - kb - 1)] = work[cols(kb), cols(kb + 1, blocks - kb - 1)]
        r_copy(kb).start()

    kb = blocks - 1
    out_copy(kb - 2).wait()
    chunk = rows // 8

    def last_copy(q):
        part = pl.ds(pl.multiple_of(q * chunk, chunk), chunk)
        return pltpu.make_async_copy(stage.at[kb % 2, part, :], modes_ref.at[part, cols(kb)], last_sem.at[q])

    @pl.loop(0, 8)
    def _(q):
        product(kb, pl.multiple_of(q * chunk, chunk), chunk)
        last_copy(q).start()

    @pl.loop(0, 8)
    def _(q):
        last_copy(q).wait()

    out_copy(kb - 1).wait()
    for i in range(blocks):
        r_copy(i).wait()


def factor_and_modes(gram, weighted):
    rows, n = weighted.shape
    vm = pl.BlockSpec(memory_space=pltpu.VMEM)
    anyspace = pl.BlockSpec(memory_space=pl.ANY)
    return pl.pallas_call(
        chol_kernel,
        name="factor_modes",
        out_shape=(jax.ShapeDtypeStruct((rows, n), F32), jax.ShapeDtypeStruct((n, n), F32)),
        in_specs=[vm, anyspace],
        out_specs=(anyspace, anyspace),
        scratch_shapes=[
            pltpu.VMEM((n, 2 * n), F32),
            pltpu.VMEM((rows, n), BF),
            pltpu.VMEM((2, 256, n), BF),
            pltpu.VMEM((2, rows, 128), F32),
            pltpu.VMEM((n, n), F32),
            pltpu.SemaphoreType.DMA((2,)),
            pltpu.SemaphoreType.DMA(()),
            pltpu.SemaphoreType.DMA((n // 128,)),
            pltpu.SemaphoreType.DMA((8,)),
        ],
    )(gram, weighted)


def on_device(snapshots, lift, adjacency, codes, obstacle):
    weighted, gram = weigh_and_gram(snapshots, lift, adjacency, codes, obstacle)
    return factor_and_modes(gram, weighted)


def solution(mesh):
    split = Mesh(
        mesh.devices.reshape(4, 4, 2, mesh.shape["tm"]), ("rows_0", "rows_1", "rows_2", "tm")
    )
    return jax.shard_map(
        on_device,
        mesh=split,
        in_specs=(P(ROWS, "tm"), P(), P(ROWS_TM, None), P(ROWS_TM, None), P(ROWS_TM)),
        out_specs=(P(ROWS_TM, None), P()),
        check_vma=False,
    )
```

```python
import functools

import jax
import jax.numpy as jnp
from jax import lax
from jax.experimental import pallas as pl
from jax.experimental.pallas import tpu as pltpu
from jax.sharding import Mesh
from jax.sharding import PartitionSpec as P

ROWS = ("rows_0", "rows_1", "rows_2")
ROWS_TM = ("rows_0", "rows_1", "rows_2", "tm")
HI = lax.Precision.HIGHEST
F32 = jnp.float32
BF = jnp.bfloat16
MESH = pl.DeviceIdType.MESH
NODES = 512
LAYER = 8 * NODES
PAIR = 2 * NODES
TILES = 1280


def at(start, size, step=8):
    return pl.ds(pl.multiple_of(start, step), size)


def halves(face):
    last = face % 2
    if face < 2:
        return last * 448, 8, 1
    if face < 4:
        return last * 56, 64, 1
    return last * 7, 64, 8


def strided(ref, start, step):
    return ref[pl.ds(start, 8), :] if step == 1 else ref[pl.ds(start, 8, stride=step), :]


def weigh_kernel(
    snap_ref, lift_hbm, adjacency_ref, codes_ref, obstacle_ref, out_ref, gram_ref,
    lift_ref, lift_sem, raw, nodes, sent, whole, table, tabs, words, smem_words, up_face, down_face, low_halo, high_halo,
    jump, gram, part, core_in, plane_in, z_in,
    load_sem, out_sem, tab_send, tab_recv, smem_sem, halo_send, halo_recv,
    send_sem, recv_sem, own_sem, core_send, core_recv, plane_send, plane_recv,
    z_send, z_recv, back_send, back_recv, pair_send, pair_recv,
):
    y, x, c, t = (lax.axis_index(n) for n in ("rows_0", "rows_1", "rows_2", "tm"))
    r = (y * 4 + x) * 2 + c
    xy = y * 4 + x

    def group(index):
        index = lax.rem(index + 32, 32)
        return (index // 8, lax.rem(index // 2, 4), lax.rem(index, 2), t)

    def plane(index):
        index = lax.rem(index, 16)
        return (index // 4, lax.rem(index, 4), c, t)

    def column(index):
        return (y, x, c, index)

    partner = (y, x, 1 - c, t)

    def remote(src, dst, send, recv, device):
        return pltpu.make_async_remote_copy(
            src_ref=src, dst_ref=dst, send_sem=send, recv_sem=recv, device_id=device, device_id_type=MESH
        )

    barrier = pltpu.get_barrier_semaphore()

    @pl.loop(1, 16)
    def _(o):
        pl.semaphore_signal(barrier, inc=1, device_id=plane(xy + o), device_id_type=MESH)

    for o in range(1, 4):
        pl.semaphore_signal(barrier, inc=1, device_id=column(lax.rem(t + o, 4)), device_id_type=MESH)
    pl.semaphore_signal(barrier, inc=1, device_id=partner, device_id_type=MESH)
    pl.semaphore_signal(
        barrier, inc=1, device_id=group(r + jnp.where(c == 1, 1, -1)), device_id_type=MESH
    )

    def load(l):
        rows = at(l * LAYER, LAYER)
        return pltpu.make_async_copy(snap_ref.at[rows, :], raw.at[rows, :], load_sem.at[l])

    for l in (3, 0, 1, 2):
        load(l).start()
    bring_lift = pltpu.make_async_copy(lift_hbm, lift_ref, lift_sem)
    bring_lift.start()

    sub = lax.broadcasted_iota(jnp.int32, (8, 128), 0)
    blocked = jnp.zeros((8, 128), jnp.int32)
    for i in range(8):
        blocked = jnp.where(sub == i, obstacle_ref[i], blocked)
    table[...] = jnp.zeros_like(table)
    table[0, :, 0:6] = adjacency_ref[...]
    table[1, :, 0:6] = codes_ref[...]
    table[2] = blocked

    def widen(l):
        load(l).wait()

        @pl.loop(0, LAYER // 256)
        def _(i):
            nodes[at((l + 1) * LAYER + i * 256, 256), :] = raw[at(l * LAYER + i * 256, 256), :].astype(F32)

    def take_face(l, face, buffer):
        @pl.loop(0, 8)
        def _(i):
            for h in range(4):
                base = (l + 1) * LAYER + i * 512 + h * 128 + face
                two = [nodes[pl.ds(base + 64 * g, 8, stride=8), :] for g in range(2)]
                buffer[at(i * 64 + h * 16, 16, 16), :] = jnp.concatenate(two, axis=0).astype(BF)

    def tab_copy(o):
        return remote(table, tabs.at[t], tab_send.at[o - 1], tab_recv.at[t], column(lax.rem(t + o, 4)))

    up = remote(up_face, low_halo, halo_send.at[0], halo_recv.at[0], group(r + 1))
    down = remote(down_face, high_halo, halo_send.at[1], halo_recv.at[1], group(r - 1))
    mine = pltpu.make_async_copy(table, tabs.at[t], own_sem.at[8])
    mine.start()
    pl.semaphore_wait(barrier, 20)
    for o in (2, 1, 3):
        tab_copy(o).start()
    widen(3)
    take_face(3, 7, up_face)
    up.start()
    widen(0)
    take_face(0, 0, down_face)
    down.start()
    widen(1)
    widen(2)
    mine.wait()
    for o in range(1, 4):
        src = lax.rem(t + o, 4)
        remote(table, tabs.at[src], tab_send.at[o - 1], tab_recv.at[src], column(src)).wait_recv()
    lane = lax.broadcasted_iota(jnp.int32, (8, 128), 1)
    merged = jnp.zeros((8, 128), jnp.int32)
    for l in range(4):
        found, code, stop = tabs[l, 0], tabs[l, 1], tabs[l, 2]
        word = (found & 7) + 8 * code + jnp.where(found < 0, 32, 0) + 64 * stop
        merged = merged + pltpu.roll(jnp.where(lane < 6, word, 0), 8 * l, 1)
    words[...] = merged
    to_smem = pltpu.make_async_copy(words, smem_words, smem_sem)
    to_smem.start()
    to_smem.wait()

    def split_step(s):
        o = lax.rem(s, 3)
        odd = lax.rem(t, 2)
        other = jnp.where(o == 0, 1 + odd, jnp.where(o == 1, 3 * (1 - odd), lax.rem(t + 2, 4)))
        return jnp.where(s < 12, s // 3, s - 12), jnp.where(s < 12, other, t)

    def layer_copy(e, l):
        return remote(
            sent.at[at(l * LAYER + e * NODES, NODES), :],
            whole.at[at(e * NODES, NODES), at(t * 128, 128, 128)],
            send_sem.at[l, e], recv_sem.at[t, e], column(l),
        )

    def own_copy(e):
        return pltpu.make_async_copy(
            sent.at[at(t * LAYER + e * NODES, NODES), :],
            whole.at[at(e * NODES, NODES), at(t * 128, 128, 128)], own_sem.at[e],
        )

    def send_step(s):
        q, l = split_step(s)

        @pl.when(s >= 12)
        def _():
            for h in range(2):
                own_copy(2 * q + h).start()

        @pl.when(s < 12)
        def _():
            for h in range(2):
                layer_copy(2 * q + h, l).start()

    def jumps_of(s, slot):
        q, l = split_step(s)
        for h in range(2):
            e = 2 * q + h
            own = ((l + 1) * 8 + e) * NODES
            for f in range(6):
                word = smem_words[e, 8 * l + f]
                n = word & 7
                k = (word >> 3) & 3
                shift = (0, 0, 0, 0, -1, 1)[f]
                base = ((l + 1 + shift) * 8 + n) * NODES
                turn = jnp.where((k == 1) | (k == 2), 1, 0)
                odd = (k & 1) == 1
                order = jnp.where(k >= 2, 7 - sub, sub)
                wall = (word & 32) != 0
                nb_first, nb_tile, nb_sub = halves(f ^ 1)
                my_first, my_tile, my_sub = halves(f)
                done = []
                for i in range(8):
                    j = i + turn * (7 - 2 * i)
                    straight = strided(nodes, base + nb_first + j * nb_tile, nb_sub)
                    across = strided(nodes, base + nb_first + j * nb_sub, nb_tile)
                    got = jnp.where(odd, across, straight)
                    got = jnp.take_along_axis(got, order, axis=0)
                    got = jnp.where(wall, 0.0, got)
                    done.append(got - strided(nodes, own + my_first + i * my_tile, my_sub))
                for i in range(4):
                    two = jnp.concatenate(done[2 * i : 2 * i + 2], axis=0).astype(BF)
                    jump[slot, f * 64 + 16 * i : f * 64 + 16 * i + 16, h * 128 : h * 128 + 128] = two

    def weigh(s, slot):
        q, l = split_step(s)
        damp = [1.0 - 0.5 * (smem_words[2 * q + h, 8 * l] >> 6).astype(F32) for h in range(2)]
        for m in range(4):
            lifted = jnp.dot(
                lift_ref[m * 128 : m * 128 + 128, :], jump[slot], preferred_element_type=F32
            )
            for h in range(2):
                e = 2 * q + h
                here = nodes[at(((l + 1) * 8 + e) * NODES + m * 128, 128), :]
                sent[at((l * 8 + e) * NODES + m * 128, 128), :] = (
                    damp[h] * here + lifted[:, h * 128 : h * 128 + 128]
                ).astype(BF)

    jumps_of(0, 0)
    bring_lift.wait()
    for copy, halo, layer, face in ((up, low_halo, 0, 7), (down, high_halo, 5, 0)):
        copy.wait_recv()

        @pl.loop(0, 8)
        def _(i):
            for h in range(4):
                two = halo[at(i * 64 + h * 16, 16, 16), :].astype(F32)
                base = layer * LAYER + i * 512 + h * 128 + face
                nodes[pl.ds(base, 8, stride=8), :] = two[0:8]
                nodes[pl.ds(base + 64, 8, stride=8), :] = two[8:16]

    @pl.loop(0, 16)
    def _(s):
        slot = lax.rem(s, 2)
        weigh(s, slot)
        jumps_of(jnp.minimum(s + 1, 15), 1 - slot)
        send_step(s)

    TN = (((0,), (0,)), ((), ()))

    def out_copy(e):
        rows = at(e * NODES, NODES)
        return pltpu.make_async_copy(whole.at[rows, :], out_ref.at[rows, :], out_sem.at[e])

    gram[...] = jnp.zeros_like(gram)

    @pl.loop(0, 8)
    def _(e):
        own_copy(e).wait()

        @pl.loop(1, 4)
        def _(o):
            src = lax.rem(t + o, 4)
            remote(
                sent.at[at(e * NODES, NODES), :],
                whole.at[at(e * NODES, NODES), at(src * 128, 128, 128)],
                send_sem.at[src, e], recv_sem.at[src, e], column(src),
            ).wait_recv()

        out_copy(e).start()
        v = whole[at(e * NODES, NODES), :]
        for b in range(2):
            left = v[:, b * 256 : b * 256 + 256]
            gram[b * 256 : b * 256 + 256, b * 256 : 512] += lax.dot_general(
                left, v[:, b * 256 : 512], TN, preferred_element_type=F32
            )

    scale = 1.0 / (1024 * NODES)
    index = 0
    for bi in range(4):
        for bj in range(bi, 4):
            part[index * 128 : index * 128 + 128, :] = (
                gram[bi * 128 : bi * 128 + 128, bj * 128 : bj * 128 + 128] * scale
            )
            index += 1

    HALF, PART = TILES // 2, TILES // 32
    CHUNK = HALF // 4
    keep, give = c * HALF, (1 - c) * HALF

    def core(i):
        k = lax.rem(y + i, 4)
        rows = at(k * CHUNK, CHUNK)
        return remote(
            part.at[at(give + k * CHUNK, CHUNK), :], core_in.at[rows, :], core_send.at[k], core_recv.at[k], partner
        )

    def to_owner(p):
        return remote(
            part.at[at(keep + p * PART, PART), :], plane_in.at[xy], plane_send.at[p], plane_recv.at[xy], plane(p)
        )

    def from_peer(p):
        return remote(
            part.at[at(keep, PART), :], plane_in.at[p], plane_send.at[p], plane_recv.at[p], plane(p)
        )

    for i in range(4):
        core(i).start()

    for i in range(4):
        core(i).wait_recv()
        k = lax.rem(y + i, 4)
        mine_rows = at(keep + k * CHUNK, CHUNK)
        part[mine_rows, :] = part[mine_rows, :] + core_in[at(k * CHUNK, CHUNK), :]
        for o in range(1 if i == 0 else 0, 4):
            to_owner(k * 4 + lax.rem(x + o, 4)).start()

    plane_in[xy] = part[at(keep + xy * PART, PART), :]

    @pl.loop(1, 16)
    def _(o):
        from_peer(lax.rem(xy + o, 16)).wait_recv()

    total = plane_in[0]
    for p in range(1, 16):
        total = total + plane_in[p]
    z_in[t] = total

    def to_column(o):
        dst = lax.rem(t + o, 4)
        return remote(z_in.at[t], z_in.at[t], z_send.at[o - 1], z_recv.at[t], column(dst))

    for o in range(1, 4):
        to_column(o).start()
    for o in range(1, 4):
        src = lax.rem(t + o, 4)
        remote(z_in.at[src], z_in.at[src], z_send.at[o - 1], z_recv.at[src], column(src)).wait_recv()

    def own_rows(p):
        return gram_ref.at[at(keep + p * PART, PART), :]

    def back(o):
        return remote(own_rows(xy), own_rows(xy), back_send.at[o], back_recv.at[xy], plane(xy + o))

    def back_from(o):
        p = lax.rem(xy + o, 16)
        return remote(own_rows(p), own_rows(p), back_send.at[o], back_recv.at[p], plane(xy + o))

    def across_core(p):
        return remote(own_rows(p), own_rows(p), pair_send.at[p], pair_recv.at[p], partner)

    def across_core_in(p):
        rows = gram_ref.at[at(give + p * PART, PART), :]
        return remote(rows, rows, pair_send.at[p], pair_recv.at[p], partner)

    gram_ref[at(keep + xy * PART, PART), :] = (z_in[0] + z_in[1]) + (z_in[2] + z_in[3])

    @pl.loop(1, 16)
    def _(o):
        back(o).start()

    across_core(xy).start()

    @pl.loop(1, 16)
    def _(o):
        back_from(o).wait_recv()
        across_core(lax.rem(xy + o, 16)).start()

    @pl.loop(0, 16)
    def _(p):
        across_core_in(p).wait_recv()

    for o in range(1, 4):
        tab_copy(o).wait_send()
        to_column(o).wait_send()
    up.wait_send()
    down.wait_send()
    for i in range(4):
        core(i).wait_send()

    @pl.loop(0, 12)
    def _(s):
        q, l = split_step(s)
        for h in range(2):
            layer_copy(2 * q + h, l).wait_send()

    @pl.loop(1, 16)
    def _(o):
        to_owner(lax.rem(xy + o, 16)).wait_send()
        back(o).wait_send()

    @pl.loop(0, 16)
    def _(p):
        across_core(p).wait_send()

    @pl.loop(0, 8)
    def _(e):
        out_copy(e).wait()


def weigh_and_gram(snapshots, lift, adjacency, codes, obstacle):
    vm = pl.BlockSpec(memory_space=pltpu.VMEM)
    sm = pl.BlockSpec(memory_space=pltpu.SMEM)
    anyspace = pl.BlockSpec(memory_space=pl.ANY)
    D = pltpu.SemaphoreType.DMA
    V = pltpu.VMEM
    I32 = jnp.int32
    return pl.pallas_call(
        weigh_kernel,
        name="weigh_gram",
        out_shape=(jax.ShapeDtypeStruct((LAYER, 512), BF), jax.ShapeDtypeStruct((TILES, 128), F32)),
        in_specs=[anyspace, anyspace, vm, vm, sm],
        out_specs=(anyspace, vm),
        scratch_shapes=[
            V((NODES, 384), BF), D(()), V((4 * LAYER, 128), BF), V((6 * LAYER, 128), F32), V((4 * LAYER, 128), BF), V((LAYER, 512), BF),
            V((3, 8, 128), I32), V((4, 3, 8, 128), I32), V((8, 128), I32), pltpu.SMEM((8, 128), I32),
            V((NODES, 128), BF), V((NODES, 128), BF), V((NODES, 128), BF), V((NODES, 128), BF),
            V((2, 384, 256), BF), V((512, 512), F32), V((TILES, 128), F32), V((TILES // 2, 128), F32),
            V((16, TILES // 32, 128), F32), V((4, TILES // 32, 128), F32),
            D((4,)), D((8,)), D((3,)), D((4,)), D(()), D((2,)), D((2,)),
            D((4, 8)), D((4, 8)), D((9,)), D((4,)), D((4,)), D((16,)), D((16,)),
            D((3,)), D((4,)), D((16,)), D((16,)), D((16,)), D((16,)),
        ],
        compiler_params=pltpu.CompilerParams(collective_id=0, has_side_effects=True),
    )(snapshots, lift, adjacency, codes, obstacle)


NEAR = 2


def lanes_of(x, lane):
    return jnp.broadcast_to(x[:, lane : lane + 1], x.shape)


def row_of(x, row):
    return jnp.broadcast_to(x[row : row + 1, :], x.shape)


def tree_sum(terms):
    while len(terms) > 1:
        terms = [terms[i] + terms[i + 1] for i in range(0, len(terms), 2)]
    return terms[0]


def eliminate(c, pivot, s, follow=None):
    sub = lax.broadcasted_iota(jnp.int32, (8, 128), 0)
    lane = lax.broadcasted_iota(jnp.int32, (8, 128), 1)
    row = pivot
    if follow:
        l, c2, nxt = follow
    for j in range(8):
        d = row_of(c[j], j)
        inv = 1.0 / d
        scale = lax.rsqrt(d)
        here, unit = sub == j, lane == s + j
        m = jnp.where(here, -inv, c[j] * inv)
        pivot = jnp.where(unit, jnp.where(here, 1.0, 0.0), pivot)
        q = row_of(pivot, j)
        row = jnp.where(here, q * scale, row)
        pivot = jnp.where(here, 0.0, pivot) - m * q
        heads = {k: row_of(c[k], j) for k in range(j + 1, 8)}
        for k in range(j + 1, 8):
            c[k] = jnp.where(here, 0.0, c[k]) - m * heads[k]
        if follow:
            ml = l[j] * inv
            nxt = jnp.where(unit, 0.0, nxt) - ml * q
            for k in range(8):
                c2[k] = c2[k] - ml * row_of(l[j], k)
            for k in range(j + 1, 8):
                l[k] = l[k] - ml * heads[k]
    return pivot, row, nxt if follow else None


def factor_block(a, beside):
    tiles = len(a)
    lane = lax.broadcasted_iota(jnp.int32, (8, 128), 1)
    rows = []
    for p in range(0, tiles, 2):
        s = 8 * p
        c = [lanes_of(a[p], s + j) for j in range(8)]
        l = [lanes_of(a[p + 1], s + j) for j in range(8)]
        c2 = [lanes_of(a[p + 1], s + 8 + j) for j in range(8)]
        far = p + 2 + NEAR
        near = range(p + 2, min(far, tiles))
        old = {i: [lanes_of(a[i], s + j) for j in range(16)] for i in near}
        q1, row, nxt = eliminate(c, a[p], s, (l, c2, a[p + 1]))
        rows.append(row)
        beside(p)
        u = [lanes_of(q1, s + 8 + j) for j in range(8)]
        q2, row, _ = eliminate(c2, nxt, s + 8)
        rows.append(row)
        beside(p + 1)
        if p + 2 == tiles:
            break
        heads = [row_of(q2, j) for j in range(8)]
        q1 = jnp.where((lane >= s + 8) & (lane < s + 16), 0.0, q1) - tree_sum([u[j] * heads[j] for j in range(8)])
        band = (lane >= s) & (lane < s + 16)
        if far < tiles:
            left = jnp.concatenate([a[i][:, s : s + 16] for i in range(far, tiles)], axis=0)
            prod = jnp.dot(left, jnp.concatenate([q1, q2], axis=0), precision=HI, preferred_element_type=F32)
        heads = [row_of(q1, j) for j in range(8)] + heads
        for i in near:
            a[i] = jnp.where(band, 0.0, a[i]) - tree_sum([old[i][j] * heads[j] for j in range(16)])
        for i in range(far, tiles):
            at = 8 * (i - far)
            a[i] = jnp.where(band, 0.0, a[i]) - prod[at : at + 8, :]
    return rows


def chol_kernel(g_ref, w_hbm, modes_ref, r_ref, work, w_ref, inv, stage, r_rows, sem, w_sem, r_sem, last_sem):
    n = r_ref.shape[1]
    blocks = n // 128
    rows = w_ref.shape[0]
    piece = rows // 16
    bring = pltpu.make_async_copy(w_hbm, w_ref, w_sem)
    bring.start()
    sub = lax.broadcasted_iota(jnp.int32, (8, 128), 0)
    lane = lax.broadcasted_iota(jnp.int32, (8, 128), 1)
    NT = (((1,), (1,)), ((), ()))
    order = [(i, j) for i in range(blocks) for j in range(i, blocks)]

    def cols(j, count=1):
        return pl.ds(j * 128, count * 128)

    for index, (i, j) in enumerate(order):
        work[cols(i), cols(j)] = g_ref[cols(index), :]
    for i in range(1, blocks):
        work[cols(i), cols(blocks, i)] = jnp.zeros((128, i * 128), F32)

    def finish(kb, window):
        work[cols(kb), window] = jnp.dot(
            work[cols(kb), cols(kb + blocks)], work[cols(kb), window], precision=HI, preferred_element_type=F32
        )

    def update(kb, i, window):
        left = work[cols(kb), cols(i)].T
        work[cols(i), window] = work[cols(i), window] - jnp.dot(
            left, work[cols(kb), window], precision=HI, preferred_element_type=F32
        )

    def keep(kb):
        depth = (kb + 1) * 128
        row = work[cols(kb), pl.ds(n, depth)]
        high = row.astype(BF)
        inv[kb % 2, 0:128, 0:depth] = high
        inv[kb % 2, 128:256, 0:depth] = (row - high.astype(F32)).astype(BF)
        if kb > 0:
            r_rows[cols(kb), cols(0, kb)] = jnp.zeros((128, kb * 128), F32)
        if kb + 1 < blocks:
            r_rows[cols(kb), cols(kb + 1, blocks - kb - 1)] = work[cols(kb), cols(kb + 1, blocks - kb - 1)]
        r_copy(kb).start()

    def product(kb, first, count):
        depth = (kb + 1) * 128
        x = w_ref[pl.ds(first, count), 0:depth]
        both = lax.dot_general(x, inv[kb % 2, :, 0:depth], NT, preferred_element_type=F32)
        stage[kb % 2, pl.ds(first, count), :] = both[:, 0:128] + both[:, 128:256]

    def out_copy(kb):
        return pltpu.make_async_copy(stage.at[kb % 2], modes_ref.at[:, cols(kb)], sem.at[kb % 2])

    def r_copy(kb):
        return pltpu.make_async_copy(r_rows.at[cols(kb), :], r_ref.at[cols(kb), :], r_sem.at[kb])

    for kb in range(blocks):
        waiting = []
        if kb >= 1:
            prev = kb - 1
            waiting = [
                [functools.partial(finish, prev, pl.ds((prev + 2) * 128, n - 256))],
                [functools.partial(keep, prev)],
                [functools.partial(update, prev, kb, pl.ds((kb + 1) * 128, n - 128))],
            ]
            for i in range(kb + 1, blocks):
                waiting.append([functools.partial(update, prev, i, pl.ds(i * 128, n + (kb - i) * 128))])
            waiting += [[] for _ in range(16 - len(waiting))]
            for q in range(16):
                waiting[min(q + 2, 15 - q % 2)].append(functools.partial(product, prev, q * piece, piece))

        def beside(p):
            if waiting:
                for task in waiting[p]:
                    task()

        if kb == 1:
            bring.wait()
        if kb >= 3:
            out_copy(kb - 3).wait()
        a = [work[pl.ds(kb * 128 + 8 * i, 8), cols(kb)] for i in range(16)]
        for i, row in enumerate(factor_block(a, beside)):
            here = pl.ds(kb * 128 + 8 * i, 8)
            diagonal, left = lane == sub + 8 * i, lane <= sub + 8 * i
            r_rows[here, cols(kb)] = jnp.where(left, jnp.where(diagonal, 1.0 / row, 0.0), row)
            work[here, cols(kb + blocks)] = jnp.where(left, row, 0.0)
        if kb >= 1:
            out_copy(kb - 1).start()
        if kb + 1 < blocks:
            finish(kb, cols(kb + 1))
            update(kb, kb + 1, cols(kb + 1))
        else:
            finish(kb, cols(kb + 1, blocks - 1))
            keep(kb)

    kb = blocks - 1
    out_copy(kb - 2).wait()
    chunk = rows // 8

    def last_copy(q):
        part = pl.ds(pl.multiple_of(q * chunk, chunk), chunk)
        return pltpu.make_async_copy(stage.at[kb % 2, part, :], modes_ref.at[part, cols(kb)], last_sem.at[q])

    @pl.loop(0, 8)
    def _(q):
        product(kb, pl.multiple_of(q * chunk, chunk), chunk)
        last_copy(q).start()

    @pl.loop(0, 8)
    def _(q):
        last_copy(q).wait()

    out_copy(kb - 1).wait()
    for i in range(blocks):
        r_copy(i).wait()


def factor_and_modes(gram, weighted):
    rows, n = weighted.shape
    vm = pl.BlockSpec(memory_space=pltpu.VMEM)
    anyspace = pl.BlockSpec(memory_space=pl.ANY)
    return pl.pallas_call(
        chol_kernel,
        name="factor_modes",
        out_shape=(jax.ShapeDtypeStruct((rows, n), F32), jax.ShapeDtypeStruct((n, n), F32)),
        in_specs=[vm, anyspace],
        out_specs=(anyspace, anyspace),
        scratch_shapes=[
            pltpu.VMEM((n, 2 * n), F32),
            pltpu.VMEM((rows, n), BF),
            pltpu.VMEM((2, 256, n), BF),
            pltpu.VMEM((2, rows, 128), F32),
            pltpu.VMEM((n, n), F32),
            pltpu.SemaphoreType.DMA((2,)),
            pltpu.SemaphoreType.DMA(()),
            pltpu.SemaphoreType.DMA((n // 128,)),
            pltpu.SemaphoreType.DMA((8,)),
        ],
        compiler_params=pltpu.CompilerParams(),
    )(gram, weighted)


def on_device(snapshots, lift, adjacency, codes, obstacle):
    weighted, gram = weigh_and_gram(snapshots, lift, adjacency, codes, obstacle)
    return factor_and_modes(gram, weighted)


def solution(mesh):
    split = Mesh(
        mesh.devices.reshape(4, 4, 2, mesh.shape["tm"]), ("rows_0", "rows_1", "rows_2", "tm")
    )
    return jax.shard_map(
        on_device,
        mesh=split,
        in_specs=(P(ROWS, "tm"), P(), P(ROWS_TM, None), P(ROWS_TM, None), P(ROWS_TM)),
        out_specs=(P(ROWS_TM, None), P()),
        check_vma=False,
    )
```

```python
import functools

import jax
import jax.numpy as jnp
from jax import lax
from jax.experimental import pallas as pl
from jax.experimental.pallas import tpu as pltpu
from jax.sharding import Mesh
from jax.sharding import PartitionSpec as P

ROWS = ("rows_0", "rows_1", "rows_2")
ROWS_TM = ("rows_0", "rows_1", "rows_2", "tm")
HI = lax.Precision.HIGHEST
F32 = jnp.float32
BF = jnp.bfloat16
MESH = pl.DeviceIdType.MESH
NODES = 512
LAYER = 8 * NODES
PAIR = 2 * NODES
TILES = 1280


def at(start, size, step=8):
    return pl.ds(pl.multiple_of(start, step), size)


def halves(face):
    last = face % 2
    if face < 2:
        return last * 448, 8, 1
    if face < 4:
        return last * 56, 64, 1
    return last * 7, 64, 8


def strided(ref, start, step):
    return ref[pl.ds(start, 8), :] if step == 1 else ref[pl.ds(start, 8, stride=step), :]


def weigh_kernel(
    snap_ref, lift_hbm, adjacency_ref, codes_ref, obstacle_ref, out_ref, gram_ref,
    lift_ref, lift_sem, raw, nodes, sent, whole, table, tabs, words, smem_words, up_face, down_face, low_halo, high_halo,
    jump, gram, part, core_in, plane_in, z_in,
    load_sem, out_sem, tab_send, tab_recv, smem_sem, halo_send, halo_recv,
    send_sem, recv_sem, own_sem, core_send, core_recv, plane_send, plane_recv,
    z_send, z_recv, back_send, back_recv, pair_send, pair_recv,
):
    y, x, c, t = (lax.axis_index(n) for n in ("rows_0", "rows_1", "rows_2", "tm"))
    r = (y * 4 + x) * 2 + c
    xy = y * 4 + x

    def group(index):
        index = lax.rem(index + 32, 32)
        return (index // 8, lax.rem(index // 2, 4), lax.rem(index, 2), t)

    def plane(index):
        index = lax.rem(index, 16)
        return (index // 4, lax.rem(index, 4), c, t)

    def column(index):
        return (y, x, c, index)

    partner = (y, x, 1 - c, t)

    def remote(src, dst, send, recv, device):
        return pltpu.make_async_remote_copy(
            src_ref=src, dst_ref=dst, send_sem=send, recv_sem=recv, device_id=device, device_id_type=MESH
        )

    barrier = pltpu.get_barrier_semaphore()

    @pl.loop(1, 16)
    def _(o):
        pl.semaphore_signal(barrier, inc=1, device_id=plane(xy + o), device_id_type=MESH)

    for o in range(1, 4):
        pl.semaphore_signal(barrier, inc=1, device_id=column(lax.rem(t + o, 4)), device_id_type=MESH)
    pl.semaphore_signal(barrier, inc=1, device_id=partner, device_id_type=MESH)
    pl.semaphore_signal(
        barrier, inc=1, device_id=group(r + jnp.where(c == 1, 1, -1)), device_id_type=MESH
    )

    def load(l):
        rows = at(l * LAYER, LAYER)
        return pltpu.make_async_copy(snap_ref.at[rows, :], raw.at[rows, :], load_sem.at[l])

    for l in (3, 0, 1, 2):
        load(l).start()
    bring_lift = pltpu.make_async_copy(lift_hbm, lift_ref, lift_sem)
    bring_lift.start()

    sub = lax.broadcasted_iota(jnp.int32, (8, 128), 0)
    blocked = jnp.zeros((8, 128), jnp.int32)
    for i in range(8):
        blocked = jnp.where(sub == i, obstacle_ref[i], blocked)
    table[...] = jnp.zeros_like(table)
    table[0, :, 0:6] = adjacency_ref[...]
    table[1, :, 0:6] = codes_ref[...]
    table[2] = blocked

    def widen(l):
        load(l).wait()

        @pl.loop(0, LAYER // 256)
        def _(i):
            nodes[at((l + 1) * LAYER + i * 256, 256), :] = raw[at(l * LAYER + i * 256, 256), :].astype(F32)

    def take_face(l, face, buffer):
        @pl.loop(0, 8)
        def _(i):
            for h in range(4):
                base = (l + 1) * LAYER + i * 512 + h * 128 + face
                two = [nodes[pl.ds(base + 64 * g, 8, stride=8), :] for g in range(2)]
                buffer[at(i * 64 + h * 16, 16, 16), :] = jnp.concatenate(two, axis=0).astype(BF)

    def tab_copy(o):
        return remote(table, tabs.at[t], tab_send.at[o - 1], tab_recv.at[t], column(lax.rem(t + o, 4)))

    up = remote(up_face, low_halo, halo_send.at[0], halo_recv.at[0], group(r + 1))
    down = remote(down_face, high_halo, halo_send.at[1], halo_recv.at[1], group(r - 1))
    mine = pltpu.make_async_copy(table, tabs.at[t], own_sem.at[8])
    mine.start()
    pl.semaphore_wait(barrier, 20)
    for o in (2, 1, 3):
        tab_copy(o).start()
    widen(3)
    take_face(3, 7, up_face)
    up.start()
    widen(0)
    take_face(0, 0, down_face)
    down.start()
    widen(1)
    widen(2)
    mine.wait()
    for o in range(1, 4):
        src = lax.rem(t + o, 4)
        remote(table, tabs.at[src], tab_send.at[o - 1], tab_recv.at[src], column(src)).wait_recv()
    lane = lax.broadcasted_iota(jnp.int32, (8, 128), 1)
    merged = jnp.zeros((8, 128), jnp.int32)
    for l in range(4):
        found, code, stop = tabs[l, 0], tabs[l, 1], tabs[l, 2]
        word = (found & 7) + 8 * code + jnp.where(found < 0, 32, 0) + 64 * stop
        merged = merged + pltpu.roll(jnp.where(lane < 6, word, 0), 8 * l, 1)
    words[...] = merged
    to_smem = pltpu.make_async_copy(words, smem_words, smem_sem)
    to_smem.start()
    to_smem.wait()

    def split_step(s):
        o = lax.rem(s, 3)
        odd = lax.rem(t, 2)
        other = jnp.where(o == 0, 1 + odd, jnp.where(o == 1, 3 * (1 - odd), lax.rem(t + 2, 4)))
        return jnp.where(s < 12, s // 3, s - 12), jnp.where(s < 12, other, t)

    def layer_copy(e, l):
        return remote(
            sent.at[at(l * LAYER + e * NODES, NODES), :],
            whole.at[at(e * NODES, NODES), at(t * 128, 128, 128)],
            send_sem.at[l, e], recv_sem.at[t, e], column(l),
        )

    def own_copy(e):
        return pltpu.make_async_copy(
            sent.at[at(t * LAYER + e * NODES, NODES), :],
            whole.at[at(e * NODES, NODES), at(t * 128, 128, 128)], own_sem.at[e],
        )

    def send_step(s):
        q, l = split_step(s)

        @pl.when(s >= 12)
        def _():
            for h in range(2):
                own_copy(2 * q + h).start()

        @pl.when(s < 12)
        def _():
            for h in range(2):
                layer_copy(2 * q + h, l).start()

    def jumps_of(s, slot):
        q, l = split_step(s)
        for h in range(2):
            e = 2 * q + h
            own = ((l + 1) * 8 + e) * NODES
            for f in range(6):
                word = smem_words[e, 8 * l + f]
                n = word & 7
                k = (word >> 3) & 3
                shift = (0, 0, 0, 0, -1, 1)[f]
                base = ((l + 1 + shift) * 8 + n) * NODES
                turn = jnp.where((k == 1) | (k == 2), 1, 0)
                odd = (k & 1) == 1
                order = jnp.where(k >= 2, 7 - sub, sub)
                wall = (word & 32) != 0
                nb_first, nb_tile, nb_sub = halves(f ^ 1)
                my_first, my_tile, my_sub = halves(f)
                done = []
                for i in range(8):
                    j = i + turn * (7 - 2 * i)
                    straight = strided(nodes, base + nb_first + j * nb_tile, nb_sub)
                    across = strided(nodes, base + nb_first + j * nb_sub, nb_tile)
                    got = jnp.where(odd, across, straight)
                    got = jnp.take_along_axis(got, order, axis=0)
                    got = jnp.where(wall, 0.0, got)
                    done.append(got - strided(nodes, own + my_first + i * my_tile, my_sub))
                for i in range(4):
                    two = jnp.concatenate(done[2 * i : 2 * i + 2], axis=0).astype(BF)
                    jump[slot, f * 64 + 16 * i : f * 64 + 16 * i + 16, h * 128 : h * 128 + 128] = two

    def weigh(s, slot):
        q, l = split_step(s)
        damp = [1.0 - 0.5 * (smem_words[2 * q + h, 8 * l] >> 6).astype(F32) for h in range(2)]
        for m in range(4):
            lifted = jnp.dot(
                lift_ref[m * 128 : m * 128 + 128, :], jump[slot], preferred_element_type=F32
            )
            for h in range(2):
                e = 2 * q + h
                here = nodes[at(((l + 1) * 8 + e) * NODES + m * 128, 128), :]
                sent[at((l * 8 + e) * NODES + m * 128, 128), :] = (
                    damp[h] * here + lifted[:, h * 128 : h * 128 + 128]
                ).astype(BF)

    jumps_of(0, 0)
    bring_lift.wait()
    for copy, halo, layer, face in ((up, low_halo, 0, 7), (down, high_halo, 5, 0)):
        copy.wait_recv()

        @pl.loop(0, 8)
        def _(i):
            for h in range(4):
                two = halo[at(i * 64 + h * 16, 16, 16), :].astype(F32)
                base = layer * LAYER + i * 512 + h * 128 + face
                nodes[pl.ds(base, 8, stride=8), :] = two[0:8]
                nodes[pl.ds(base + 64, 8, stride=8), :] = two[8:16]

    @pl.loop(0, 16)
    def _(s):
        slot = lax.rem(s, 2)
        weigh(s, slot)
        jumps_of(jnp.minimum(s + 1, 15), 1 - slot)
        send_step(s)

    TN = (((0,), (0,)), ((), ()))

    def out_copy(e):
        rows = at(e * NODES, NODES)
        return pltpu.make_async_copy(whole.at[rows, :], out_ref.at[rows, :], out_sem.at[e])

    gram[...] = jnp.zeros_like(gram)

    @pl.loop(0, 8)
    def _(e):
        own_copy(e).wait()

        @pl.loop(1, 4)
        def _(o):
            src = lax.rem(t + o, 4)
            remote(
                sent.at[at(e * NODES, NODES), :],
                whole.at[at(e * NODES, NODES), at(src * 128, 128, 128)],
                send_sem.at[src, e], recv_sem.at[src, e], column(src),
            ).wait_recv()

        out_copy(e).start()
        v = whole[at(e * NODES, NODES), :]
        for b in range(2):
            left = v[:, b * 256 : b * 256 + 256]
            gram[b * 256 : b * 256 + 256, b * 256 : 512] += lax.dot_general(
                left, v[:, b * 256 : 512], TN, preferred_element_type=F32
            )

    scale = 1.0 / (1024 * NODES)
    index = 0
    for bi in range(4):
        for bj in range(bi, 4):
            part[index * 128 : index * 128 + 128, :] = (
                gram[bi * 128 : bi * 128 + 128, bj * 128 : bj * 128 + 128] * scale
            )
            index += 1

    HALF, PART = TILES // 2, TILES // 32
    CHUNK = HALF // 4
    keep, give = c * HALF, (1 - c) * HALF

    def core(i):
        k = lax.rem(y + i, 4)
        rows = at(k * CHUNK, CHUNK)
        return remote(
            part.at[at(give + k * CHUNK, CHUNK), :], core_in.at[rows, :], core_send.at[k], core_recv.at[k], partner
        )

    def to_owner(p):
        return remote(
            part.at[at(keep + p * PART, PART), :], plane_in.at[xy], plane_send.at[p], plane_recv.at[xy], plane(p)
        )

    def from_peer(p):
        return remote(
            part.at[at(keep, PART), :], plane_in.at[p], plane_send.at[p], plane_recv.at[p], plane(p)
        )

    for i in range(4):
        core(i).start()

    for i in range(4):
        core(i).wait_recv()
        k = lax.rem(y + i, 4)
        mine_rows = at(keep + k * CHUNK, CHUNK)
        part[mine_rows, :] = part[mine_rows, :] + core_in[at(k * CHUNK, CHUNK), :]
        for o in range(1 if i == 0 else 0, 4):
            to_owner(k * 4 + lax.rem(x + o, 4)).start()

    plane_in[xy] = part[at(keep + xy * PART, PART), :]

    @pl.loop(1, 16)
    def _(o):
        from_peer(lax.rem(xy + o, 16)).wait_recv()

    total = plane_in[0]
    for p in range(1, 16):
        total = total + plane_in[p]
    z_in[t] = total

    def to_column(o):
        dst = lax.rem(t + o, 4)
        return remote(z_in.at[t], z_in.at[t], z_send.at[o - 1], z_recv.at[t], column(dst))

    for o in range(1, 4):
        to_column(o).start()
    for o in range(1, 4):
        src = lax.rem(t + o, 4)
        remote(z_in.at[src], z_in.at[src], z_send.at[o - 1], z_recv.at[src], column(src)).wait_recv()

    def own_rows(p):
        return gram_ref.at[at(keep + p * PART, PART), :]

    def back(o):
        return remote(own_rows(xy), own_rows(xy), back_send.at[o], back_recv.at[xy], plane(xy + o))

    def back_from(o):
        p = lax.rem(xy + o, 16)
        return remote(own_rows(p), own_rows(p), back_send.at[o], back_recv.at[p], plane(xy + o))

    def across_core(p):
        return remote(own_rows(p), own_rows(p), pair_send.at[p], pair_recv.at[p], partner)

    def across_core_in(p):
        rows = gram_ref.at[at(give + p * PART, PART), :]
        return remote(rows, rows, pair_send.at[p], pair_recv.at[p], partner)

    gram_ref[at(keep + xy * PART, PART), :] = (z_in[0] + z_in[1]) + (z_in[2] + z_in[3])

    @pl.loop(1, 16)
    def _(o):
        back(o).start()

    across_core(xy).start()

    @pl.loop(1, 16)
    def _(o):
        back_from(o).wait_recv()
        across_core(lax.rem(xy + o, 16)).start()

    @pl.loop(0, 16)
    def _(p):
        across_core_in(p).wait_recv()

    for o in range(1, 4):
        tab_copy(o).wait_send()
        to_column(o).wait_send()
    up.wait_send()
    down.wait_send()
    for i in range(4):
        core(i).wait_send()

    @pl.loop(0, 12)
    def _(s):
        q, l = split_step(s)
        for h in range(2):
            layer_copy(2 * q + h, l).wait_send()

    @pl.loop(1, 16)
    def _(o):
        to_owner(lax.rem(xy + o, 16)).wait_send()
        back(o).wait_send()

    @pl.loop(0, 16)
    def _(p):
        across_core(p).wait_send()

    @pl.loop(0, 8)
    def _(e):
        out_copy(e).wait()


def weigh_and_gram(snapshots, lift, adjacency, codes, obstacle):
    vm = pl.BlockSpec(memory_space=pltpu.VMEM)
    sm = pl.BlockSpec(memory_space=pltpu.SMEM)
    anyspace = pl.BlockSpec(memory_space=pl.ANY)
    D = pltpu.SemaphoreType.DMA
    V = pltpu.VMEM
    I32 = jnp.int32
    return pl.pallas_call(
        weigh_kernel,
        name="weigh_gram",
        out_shape=(jax.ShapeDtypeStruct((LAYER, 512), BF), jax.ShapeDtypeStruct((TILES, 128), F32)),
        in_specs=[anyspace, anyspace, vm, vm, sm],
        out_specs=(anyspace, vm),
        scratch_shapes=[
            V((NODES, 384), BF), D(()), V((4 * LAYER, 128), BF), V((6 * LAYER, 128), F32), V((4 * LAYER, 128), BF), V((LAYER, 512), BF),
            V((3, 8, 128), I32), V((4, 3, 8, 128), I32), V((8, 128), I32), pltpu.SMEM((8, 128), I32),
            V((NODES, 128), BF), V((NODES, 128), BF), V((NODES, 128), BF), V((NODES, 128), BF),
            V((2, 384, 256), BF), V((512, 512), F32), V((TILES, 128), F32), V((TILES // 2, 128), F32),
            V((16, TILES // 32, 128), F32), V((4, TILES // 32, 128), F32),
            D((4,)), D((8,)), D((3,)), D((4,)), D(()), D((2,)), D((2,)),
            D((4, 8)), D((4, 8)), D((9,)), D((4,)), D((4,)), D((16,)), D((16,)),
            D((3,)), D((4,)), D((16,)), D((16,)), D((16,)), D((16,)),
        ],
        compiler_params=pltpu.CompilerParams(collective_id=0, has_side_effects=True),
    )(snapshots, lift, adjacency, codes, obstacle)


NEAR = 2


def lanes_of(x, lane):
    return jnp.broadcast_to(x[:, lane : lane + 1], x.shape)


def row_of(x, row):
    return jnp.broadcast_to(x[row : row + 1, :], x.shape)


def tree_sum(terms):
    while len(terms) > 1:
        terms = [terms[i] + terms[i + 1] for i in range(0, len(terms), 2)]
    return terms[0]


def eliminate(c, pivot, s, follow=None):
    sub = lax.broadcasted_iota(jnp.int32, (8, 128), 0)
    lane = lax.broadcasted_iota(jnp.int32, (8, 128), 1)
    row = pivot
    if follow:
        l, c2, nxt = follow
    for j in range(8):
        d = row_of(c[j], j)
        inv = 1.0 / d
        scale = lax.rsqrt(d)
        here, unit = sub == j, lane == s + j
        m = jnp.where(here, -inv, c[j] * inv)
        pivot = jnp.where(unit, jnp.where(here, 1.0, 0.0), pivot)
        q = row_of(pivot, j)
        row = jnp.where(here, q * scale, row)
        pivot = jnp.where(here, 0.0, pivot) - m * q
        heads = {k: row_of(c[k], j) for k in range(j + 1, 8)}
        for k in range(j + 1, 8):
            c[k] = jnp.where(here, 0.0, c[k]) - m * heads[k]
        if follow:
            ml = l[j] * inv
            nxt = jnp.where(unit, 0.0, nxt) - ml * q
            for k in range(8):
                c2[k] = c2[k] - ml * row_of(l[j], k)
            for k in range(j + 1, 8):
                l[k] = l[k] - ml * heads[k]
    return pivot, row, nxt if follow else None


def factor_block(a, beside):
    tiles = len(a)
    lane = lax.broadcasted_iota(jnp.int32, (8, 128), 1)
    rows = []
    for p in range(0, tiles, 2):
        s = 8 * p
        c = [lanes_of(a[p], s + j) for j in range(8)]
        l = [lanes_of(a[p + 1], s + j) for j in range(8)]
        c2 = [lanes_of(a[p + 1], s + 8 + j) for j in range(8)]
        far = p + 2 + NEAR
        near = range(p + 2, min(far, tiles))
        old = {i: [lanes_of(a[i], s + j) for j in range(16)] for i in near}
        q1, row, nxt = eliminate(c, a[p], s, (l, c2, a[p + 1]))
        rows.append(row)
        beside(p)
        u = [lanes_of(q1, s + 8 + j) for j in range(8)]
        q2, row, _ = eliminate(c2, nxt, s + 8)
        rows.append(row)
        beside(p + 1)
        if p + 2 == tiles:
            break
        heads = [row_of(q2, j) for j in range(8)]
        q1 = jnp.where((lane >= s + 8) & (lane < s + 16), 0.0, q1) - tree_sum([u[j] * heads[j] for j in range(8)])
        band = (lane >= s) & (lane < s + 16)
        if far < tiles:
            left = jnp.concatenate([a[i][:, s : s + 16] for i in range(far, tiles)], axis=0)
            prod = jnp.dot(left, jnp.concatenate([q1, q2], axis=0), precision=HI, preferred_element_type=F32)
        heads = [row_of(q1, j) for j in range(8)] + heads
        for i in near:
            a[i] = jnp.where(band, 0.0, a[i]) - tree_sum([old[i][j] * heads[j] for j in range(16)])
        for i in range(far, tiles):
            at = 8 * (i - far)
            a[i] = jnp.where(band, 0.0, a[i]) - prod[at : at + 8, :]
    return rows


def chol_kernel(g_ref, w_hbm, modes_ref, r_ref, work, w_ref, inv, stage, r_rows, sem, w_sem, r_sem, last_sem):
    n = r_ref.shape[1]
    blocks = n // 128
    rows = w_ref.shape[0]
    piece = rows // 16
    bring = pltpu.make_async_copy(w_hbm, w_ref, w_sem)
    bring.start()
    sub = lax.broadcasted_iota(jnp.int32, (8, 128), 0)
    lane = lax.broadcasted_iota(jnp.int32, (8, 128), 1)
    NT = (((1,), (1,)), ((), ()))
    order = [(i, j) for i in range(blocks) for j in range(i, blocks)]

    def cols(j, count=1):
        return pl.ds(j * 128, count * 128)

    for index, (i, j) in enumerate(order):
        work[cols(i), cols(j)] = g_ref[cols(index), :]
    for i in range(1, blocks):
        work[cols(i), cols(blocks, i)] = jnp.zeros((128, i * 128), F32)

    def finish(kb, window):
        work[cols(kb), window] = jnp.dot(
            work[cols(kb), cols(kb + blocks)], work[cols(kb), window], precision=HI, preferred_element_type=F32
        )

    def update(kb, i, window):
        left = work[cols(kb), cols(i)].T
        work[cols(i), window] = work[cols(i), window] - jnp.dot(
            left, work[cols(kb), window], precision=HI, preferred_element_type=F32
        )

    def keep(kb):
        depth = (kb + 1) * 128
        row = work[cols(kb), pl.ds(n, depth)]
        high = row.astype(BF)
        inv[kb % 2, 0:128, 0:depth] = high
        inv[kb % 2, 128:256, 0:depth] = (row - high.astype(F32)).astype(BF)
        if kb > 0:
            r_rows[cols(kb), cols(0, kb)] = jnp.zeros((128, kb * 128), F32)
        if kb + 1 < blocks:
            r_rows[cols(kb), cols(kb + 1, blocks - kb - 1)] = work[cols(kb), cols(kb + 1, blocks - kb - 1)]
        r_copy(kb).start()

    def product(kb, first, count):
        depth = (kb + 1) * 128
        x = w_ref[pl.ds(first, count), 0:depth]
        both = lax.dot_general(x, inv[kb % 2, :, 0:depth], NT, preferred_element_type=F32)
        stage[kb % 2, pl.ds(first, count), :] = both[:, 0:128] + both[:, 128:256]

    def out_copy(kb):
        return pltpu.make_async_copy(stage.at[kb % 2], modes_ref.at[:, cols(kb)], sem.at[kb % 2])

    def r_copy(kb):
        return pltpu.make_async_copy(r_rows.at[cols(kb), :], r_ref.at[cols(kb), :], r_sem.at[kb])

    for kb in range(blocks):
        waiting = []
        if kb >= 1:
            prev = kb - 1
            waiting = [
                [functools.partial(finish, prev, pl.ds((prev + 2) * 128, n - 256))],
                [functools.partial(keep, prev)],
                [functools.partial(update, prev, kb, pl.ds((kb + 1) * 128, n - 128))],
            ]
            for i in range(kb + 1, blocks):
                waiting.append([functools.partial(update, prev, i, pl.ds(i * 128, n + (kb - i) * 128))])
            waiting += [[] for _ in range(16 - len(waiting))]
            for q in range(16):
                waiting[min(q + 2, 15 - q % 2)].append(functools.partial(product, prev, q * piece, piece))

        def beside(p):
            if waiting:
                for task in waiting[p]:
                    task()

        if kb == 1:
            bring.wait()
        if kb >= 3:
            out_copy(kb - 3).wait()
        a = [work[pl.ds(kb * 128 + 8 * i, 8), cols(kb)] for i in range(16)]
        for i, row in enumerate(factor_block(a, beside)):
            here = pl.ds(kb * 128 + 8 * i, 8)
            diagonal, left = lane == sub + 8 * i, lane <= sub + 8 * i
            r_rows[here, cols(kb)] = jnp.where(left, jnp.where(diagonal, 1.0 / row, 0.0), row)
            work[here, cols(kb + blocks)] = jnp.where(left, row, 0.0)
        if kb >= 1:
            out_copy(kb - 1).start()
        if kb + 1 < blocks:
            finish(kb, cols(kb + 1))
            update(kb, kb + 1, cols(kb + 1))
        else:
            finish(kb, cols(kb + 1, blocks - 1))
            keep(kb)

    kb = blocks - 1
    out_copy(kb - 2).wait()
    chunk = rows // 8

    def last_copy(q):
        part = pl.ds(pl.multiple_of(q * chunk, chunk), chunk)
        return pltpu.make_async_copy(stage.at[kb % 2, part, :], modes_ref.at[part, cols(kb)], last_sem.at[q])

    for q in range(8):
        product(kb, q * chunk, chunk)
        last_copy(q).start()

    @pl.loop(0, 8)
    def _(q):
        last_copy(q).wait()

    out_copy(kb - 1).wait()
    for i in range(blocks):
        r_copy(i).wait()


def factor_and_modes(gram, weighted):
    rows, n = weighted.shape
    vm = pl.BlockSpec(memory_space=pltpu.VMEM)
    anyspace = pl.BlockSpec(memory_space=pl.ANY)
    return pl.pallas_call(
        chol_kernel,
        name="factor_modes",
        out_shape=(jax.ShapeDtypeStruct((rows, n), F32), jax.ShapeDtypeStruct((n, n), F32)),
        in_specs=[vm, anyspace],
        out_specs=(anyspace, anyspace),
        scratch_shapes=[
            pltpu.VMEM((n, 2 * n), F32),
            pltpu.VMEM((rows, n), BF),
            pltpu.VMEM((2, 256, n), BF),
            pltpu.VMEM((2, rows, 128), F32),
            pltpu.VMEM((n, n), F32),
            pltpu.SemaphoreType.DMA((2,)),
            pltpu.SemaphoreType.DMA(()),
            pltpu.SemaphoreType.DMA((n // 128,)),
            pltpu.SemaphoreType.DMA((8,)),
        ],
        compiler_params=pltpu.CompilerParams(),
    )(gram, weighted)


def on_device(snapshots, lift, adjacency, codes, obstacle):
    weighted, gram = weigh_and_gram(snapshots, lift, adjacency, codes, obstacle)
    return factor_and_modes(gram, weighted)


def solution(mesh):
    split = Mesh(
        mesh.devices.reshape(4, 4, 2, mesh.shape["tm"]), ("rows_0", "rows_1", "rows_2", "tm")
    )
    return jax.shard_map(
        on_device,
        mesh=split,
        in_specs=(P(ROWS, "tm"), P(), P(ROWS_TM, None), P(ROWS_TM, None), P(ROWS_TM)),
        out_specs=(P(ROWS_TM, None), P()),
        check_vma=False,
    )
```

```python
import functools

import jax
import jax.numpy as jnp
from jax import lax
from jax.experimental import pallas as pl
from jax.experimental.pallas import tpu as pltpu
from jax.sharding import Mesh
from jax.sharding import PartitionSpec as P

ROWS = ("rows_0", "rows_1", "rows_2")
ROWS_TM = ("rows_0", "rows_1", "rows_2", "tm")
HI = lax.Precision.HIGHEST
F32 = jnp.float32
BF = jnp.bfloat16
MESH = pl.DeviceIdType.MESH
NODES = 512
LAYER = 8 * NODES
PAIR = 2 * NODES
TILES = 1280


def at(start, size, step=8):
    return pl.ds(pl.multiple_of(start, step), size)


def halves(face):
    last = face % 2
    if face < 2:
        return last * 448, 8, 1
    if face < 4:
        return last * 56, 64, 1
    return last * 7, 64, 8


def strided(ref, start, step):
    return ref[pl.ds(start, 8), :] if step == 1 else ref[pl.ds(start, 8, stride=step), :]


def weigh_kernel(
    snap_ref, lift_hbm, adjacency_ref, codes_ref, obstacle_ref, out_ref, gram_ref,
    lift_ref, lift_sem, raw, nodes, sent, whole, table, tabs, words, smem_words, up_face, down_face, low_halo, high_halo,
    jump, gram, part, core_in, plane_in, z_in,
    load_sem, out_sem, tab_send, tab_recv, smem_sem, halo_send, halo_recv,
    send_sem, recv_sem, own_sem, core_send, core_recv, plane_send, plane_recv,
    z_send, z_recv, back_send, back_recv, pair_send, pair_recv,
):
    y, x, c, t = (lax.axis_index(n) for n in ("rows_0", "rows_1", "rows_2", "tm"))
    r = (y * 4 + x) * 2 + c
    xy = y * 4 + x

    def group(index):
        index = lax.rem(index + 32, 32)
        return (index // 8, lax.rem(index // 2, 4), lax.rem(index, 2), t)

    def plane(index):
        index = lax.rem(index, 16)
        return (index // 4, lax.rem(index, 4), c, t)

    def column(index):
        return (y, x, c, index)

    partner = (y, x, 1 - c, t)

    def remote(src, dst, send, recv, device):
        return pltpu.make_async_remote_copy(
            src_ref=src, dst_ref=dst, send_sem=send, recv_sem=recv, device_id=device, device_id_type=MESH
        )

    barrier = pltpu.get_barrier_semaphore()

    @pl.loop(1, 16)
    def _(o):
        pl.semaphore_signal(barrier, inc=1, device_id=plane(xy + o), device_id_type=MESH)

    for o in range(1, 4):
        pl.semaphore_signal(barrier, inc=1, device_id=column(lax.rem(t + o, 4)), device_id_type=MESH)
    pl.semaphore_signal(barrier, inc=1, device_id=partner, device_id_type=MESH)
    pl.semaphore_signal(
        barrier, inc=1, device_id=group(r + jnp.where(c == 1, 1, -1)), device_id_type=MESH
    )

    def load(l):
        rows = at(l * LAYER, LAYER)
        return pltpu.make_async_copy(snap_ref.at[rows, :], raw.at[rows, :], load_sem.at[l])

    for l in (3, 0, 1, 2):
        load(l).start()
    bring_lift = pltpu.make_async_copy(lift_hbm, lift_ref, lift_sem)
    bring_lift.start()

    sub = lax.broadcasted_iota(jnp.int32, (8, 128), 0)
    blocked = jnp.zeros((8, 128), jnp.int32)
    for i in range(8):
        blocked = jnp.where(sub == i, obstacle_ref[i], blocked)
    table[...] = jnp.zeros_like(table)
    table[0, :, 0:6] = adjacency_ref[...]
    table[1, :, 0:6] = codes_ref[...]
    table[2] = blocked

    def widen(l):
        load(l).wait()

        @pl.loop(0, LAYER // 256)
        def _(i):
            nodes[at((l + 1) * LAYER + i * 256, 256), :] = raw[at(l * LAYER + i * 256, 256), :].astype(F32)

    def take_face(l, face, buffer):
        @pl.loop(0, 8)
        def _(i):
            for h in range(4):
                base = (l + 1) * LAYER + i * 512 + h * 128 + face
                two = [nodes[pl.ds(base + 64 * g, 8, stride=8), :] for g in range(2)]
                buffer[at(i * 64 + h * 16, 16, 16), :] = jnp.concatenate(two, axis=0).astype(BF)

    def tab_copy(o):
        return remote(table, tabs.at[t], tab_send.at[o - 1], tab_recv.at[t], column(lax.rem(t + o, 4)))

    up = remote(up_face, low_halo, halo_send.at[0], halo_recv.at[0], group(r + 1))
    down = remote(down_face, high_halo, halo_send.at[1], halo_recv.at[1], group(r - 1))
    mine = pltpu.make_async_copy(table, tabs.at[t], own_sem.at[8])
    mine.start()
    pl.semaphore_wait(barrier, 20)
    for o in (2, 1, 3):
        tab_copy(o).start()
    widen(3)
    take_face(3, 7, up_face)
    up.start()
    widen(0)
    take_face(0, 0, down_face)
    down.start()
    widen(1)
    widen(2)
    mine.wait()
    for o in range(1, 4):
        src = lax.rem(t + o, 4)
        remote(table, tabs.at[src], tab_send.at[o - 1], tab_recv.at[src], column(src)).wait_recv()
    lane = lax.broadcasted_iota(jnp.int32, (8, 128), 1)
    merged = jnp.zeros((8, 128), jnp.int32)
    for l in range(4):
        found, code, stop = tabs[l, 0], tabs[l, 1], tabs[l, 2]
        word = (found & 7) + 8 * code + jnp.where(found < 0, 32, 0) + 64 * stop
        merged = merged + pltpu.roll(jnp.where(lane < 6, word, 0), 8 * l, 1)
    words[...] = merged
    to_smem = pltpu.make_async_copy(words, smem_words, smem_sem)
    to_smem.start()
    to_smem.wait()

    def split_step(s):
        o = lax.rem(s, 3)
        odd = lax.rem(t, 2)
        other = jnp.where(o == 0, 1 + odd, jnp.where(o == 1, 3 * (1 - odd), lax.rem(t + 2, 4)))
        return jnp.where(s < 12, s // 3, s - 12), jnp.where(s < 12, other, t)

    def layer_copy(e, l):
        return remote(
            sent.at[at(l * LAYER + e * NODES, NODES), :],
            whole.at[at(e * NODES, NODES), at(t * 128, 128, 128)],
            send_sem.at[l, e], recv_sem.at[t, e], column(l),
        )

    def own_copy(e):
        return pltpu.make_async_copy(
            sent.at[at(t * LAYER + e * NODES, NODES), :],
            whole.at[at(e * NODES, NODES), at(t * 128, 128, 128)], own_sem.at[e],
        )

    def send_step(s):
        q, l = split_step(s)

        @pl.when(s >= 12)
        def _():
            for h in range(2):
                own_copy(2 * q + h).start()

        @pl.when(s < 12)
        def _():
            for h in range(2):
                layer_copy(2 * q + h, l).start()

    def jumps_of(s, slot):
        q, l = split_step(s)
        for h in range(2):
            e = 2 * q + h
            own = ((l + 1) * 8 + e) * NODES
            for f in range(6):
                word = smem_words[e, 8 * l + f]
                n = word & 7
                k = (word >> 3) & 3
                shift = (0, 0, 0, 0, -1, 1)[f]
                base = ((l + 1 + shift) * 8 + n) * NODES
                turn = jnp.where((k == 1) | (k == 2), 1, 0)
                odd = (k & 1) == 1
                order = jnp.where(k >= 2, 7 - sub, sub)
                wall = (word & 32) != 0
                nb_first, nb_tile, nb_sub = halves(f ^ 1)
                my_first, my_tile, my_sub = halves(f)
                done = []
                for i in range(8):
                    j = i + turn * (7 - 2 * i)
                    straight = strided(nodes, base + nb_first + j * nb_tile, nb_sub)
                    across = strided(nodes, base + nb_first + j * nb_sub, nb_tile)
                    got = jnp.where(odd, across, straight)
                    got = jnp.take_along_axis(got, order, axis=0)
                    got = jnp.where(wall, 0.0, got)
                    done.append(got - strided(nodes, own + my_first + i * my_tile, my_sub))
                for i in range(4):
                    two = jnp.concatenate(done[2 * i : 2 * i + 2], axis=0).astype(BF)
                    jump[slot, f * 64 + 16 * i : f * 64 + 16 * i + 16, h * 128 : h * 128 + 128] = two

    def weigh(s, slot):
        q, l = split_step(s)
        damp = [1.0 - 0.5 * (smem_words[2 * q + h, 8 * l] >> 6).astype(F32) for h in range(2)]
        for m in range(4):
            lifted = jnp.dot(
                lift_ref[m * 128 : m * 128 + 128, :], jump[slot], preferred_element_type=F32
            )
            for h in range(2):
                e = 2 * q + h
                here = nodes[at(((l + 1) * 8 + e) * NODES + m * 128, 128), :]
                sent[at((l * 8 + e) * NODES + m * 128, 128), :] = (
                    damp[h] * here + lifted[:, h * 128 : h * 128 + 128]
                ).astype(BF)

    jumps_of(0, 0)
    bring_lift.wait()
    for copy, halo, layer, face in ((up, low_halo, 0, 7), (down, high_halo, 5, 0)):
        copy.wait_recv()

        @pl.loop(0, 8)
        def _(i):
            for h in range(4):
                two = halo[at(i * 64 + h * 16, 16, 16), :].astype(F32)
                base = layer * LAYER + i * 512 + h * 128 + face
                nodes[pl.ds(base, 8, stride=8), :] = two[0:8]
                nodes[pl.ds(base + 64, 8, stride=8), :] = two[8:16]

    @pl.loop(0, 16)
    def _(s):
        slot = lax.rem(s, 2)
        weigh(s, slot)
        jumps_of(jnp.minimum(s + 1, 15), 1 - slot)
        send_step(s)

    TN = (((0,), (0,)), ((), ()))

    def out_copy(e):
        rows = at(e * NODES, NODES)
        return pltpu.make_async_copy(whole.at[rows, :], out_ref.at[rows, :], out_sem.at[e])

    gram[...] = jnp.zeros_like(gram)

    @pl.loop(0, 8)
    def _(e):
        own_copy(e).wait()

        @pl.loop(1, 4)
        def _(o):
            src = lax.rem(t + o, 4)
            remote(
                sent.at[at(e * NODES, NODES), :],
                whole.at[at(e * NODES, NODES), at(src * 128, 128, 128)],
                send_sem.at[src, e], recv_sem.at[src, e], column(src),
            ).wait_recv()

        out_copy(e).start()
        v = whole[at(e * NODES, NODES), :]
        for b in range(2):
            left = v[:, b * 256 : b * 256 + 256]
            gram[b * 256 : b * 256 + 256, b * 256 : 512] += lax.dot_general(
                left, v[:, b * 256 : 512], TN, preferred_element_type=F32
            )

    scale = 1.0 / (1024 * NODES)
    index = 0
    for bi in range(4):
        for bj in range(bi, 4):
            part[index * 128 : index * 128 + 128, :] = (
                gram[bi * 128 : bi * 128 + 128, bj * 128 : bj * 128 + 128] * scale
            )
            index += 1

    HALF, PART = TILES // 2, TILES // 32
    CHUNK = HALF // 4
    keep, give = c * HALF, (1 - c) * HALF

    def core(i):
        k = lax.rem(y + i, 4)
        rows = at(k * CHUNK, CHUNK)
        return remote(
            part.at[at(give + k * CHUNK, CHUNK), :], core_in.at[rows, :], core_send.at[k], core_recv.at[k], partner
        )

    def to_owner(p):
        return remote(
            part.at[at(keep + p * PART, PART), :], plane_in.at[xy], plane_send.at[p], plane_recv.at[xy], plane(p)
        )

    def from_peer(p):
        return remote(
            part.at[at(keep, PART), :], plane_in.at[p], plane_send.at[p], plane_recv.at[p], plane(p)
        )

    for i in range(4):
        core(i).start()

    for i in range(4):
        core(i).wait_recv()
        k = lax.rem(y + i, 4)
        mine_rows = at(keep + k * CHUNK, CHUNK)
        part[mine_rows, :] = part[mine_rows, :] + core_in[at(k * CHUNK, CHUNK), :]
        for o in range(1 if i == 0 else 0, 4):
            to_owner(k * 4 + lax.rem(x + o, 4)).start()

    plane_in[xy] = part[at(keep + xy * PART, PART), :]

    @pl.loop(1, 16)
    def _(o):
        from_peer(lax.rem(xy + o, 16)).wait_recv()

    total = plane_in[0]
    for p in range(1, 16):
        total = total + plane_in[p]
    z_in[t] = total

    def to_column(o):
        dst = lax.rem(t + o, 4)
        return remote(z_in.at[t], z_in.at[t], z_send.at[o - 1], z_recv.at[t], column(dst))

    for o in range(1, 4):
        to_column(o).start()
    for o in range(1, 4):
        src = lax.rem(t + o, 4)
        remote(z_in.at[src], z_in.at[src], z_send.at[o - 1], z_recv.at[src], column(src)).wait_recv()

    def own_rows(p):
        return gram_ref.at[at(keep + p * PART, PART), :]

    def back(o):
        return remote(own_rows(xy), own_rows(xy), back_send.at[o], back_recv.at[xy], plane(xy + o))

    def back_from(o):
        p = lax.rem(xy + o, 16)
        return remote(own_rows(p), own_rows(p), back_send.at[o], back_recv.at[p], plane(xy + o))

    def across_core(p):
        return remote(own_rows(p), own_rows(p), pair_send.at[p], pair_recv.at[p], partner)

    def across_core_in(p):
        rows = gram_ref.at[at(give + p * PART, PART), :]
        return remote(rows, rows, pair_send.at[p], pair_recv.at[p], partner)

    gram_ref[at(keep + xy * PART, PART), :] = (z_in[0] + z_in[1]) + (z_in[2] + z_in[3])

    @pl.loop(1, 16)
    def _(o):
        back(o).start()

    across_core(xy).start()

    @pl.loop(1, 16)
    def _(o):
        back_from(o).wait_recv()
        across_core(lax.rem(xy + o, 16)).start()

    @pl.loop(0, 16)
    def _(p):
        across_core_in(p).wait_recv()

    for o in range(1, 4):
        tab_copy(o).wait_send()
        to_column(o).wait_send()
    up.wait_send()
    down.wait_send()
    for i in range(4):
        core(i).wait_send()

    @pl.loop(0, 12)
    def _(s):
        q, l = split_step(s)
        for h in range(2):
            layer_copy(2 * q + h, l).wait_send()

    @pl.loop(1, 16)
    def _(o):
        to_owner(lax.rem(xy + o, 16)).wait_send()
        back(o).wait_send()

    @pl.loop(0, 16)
    def _(p):
        across_core(p).wait_send()

    @pl.loop(0, 8)
    def _(e):
        out_copy(e).wait()


def weigh_and_gram(snapshots, lift, adjacency, codes, obstacle):
    vm = pl.BlockSpec(memory_space=pltpu.VMEM)
    sm = pl.BlockSpec(memory_space=pltpu.SMEM)
    anyspace = pl.BlockSpec(memory_space=pl.ANY)
    D = pltpu.SemaphoreType.DMA
    V = pltpu.VMEM
    I32 = jnp.int32
    return pl.pallas_call(
        weigh_kernel,
        name="weigh_gram",
        out_shape=(jax.ShapeDtypeStruct((LAYER, 512), BF), jax.ShapeDtypeStruct((TILES, 128), F32)),
        in_specs=[anyspace, anyspace, vm, vm, sm],
        out_specs=(anyspace, vm),
        scratch_shapes=[
            V((NODES, 384), BF), D(()), V((4 * LAYER, 128), BF), V((6 * LAYER, 128), F32), V((4 * LAYER, 128), BF), V((LAYER, 512), BF),
            V((3, 8, 128), I32), V((4, 3, 8, 128), I32), V((8, 128), I32), pltpu.SMEM((8, 128), I32),
            V((NODES, 128), BF), V((NODES, 128), BF), V((NODES, 128), BF), V((NODES, 128), BF),
            V((2, 384, 256), BF), V((512, 512), F32), V((TILES, 128), F32), V((TILES // 2, 128), F32),
            V((16, TILES // 32, 128), F32), V((4, TILES // 32, 128), F32),
            D((4,)), D((8,)), D((3,)), D((4,)), D(()), D((2,)), D((2,)),
            D((4, 8)), D((4, 8)), D((9,)), D((4,)), D((4,)), D((16,)), D((16,)),
            D((3,)), D((4,)), D((16,)), D((16,)), D((16,)), D((16,)),
        ],
        compiler_params=pltpu.CompilerParams(collective_id=0, has_side_effects=True),
    )(snapshots, lift, adjacency, codes, obstacle)


NEAR = 2


def lanes_of(x, lane):
    return jnp.broadcast_to(x[:, lane : lane + 1], x.shape)


def row_of(x, row):
    return jnp.broadcast_to(x[row : row + 1, :], x.shape)


def tree_sum(terms):
    while len(terms) > 1:
        terms = [terms[i] + terms[i + 1] for i in range(0, len(terms), 2)]
    return terms[0]


def eliminate(c, pivot, s, follow=None):
    sub = lax.broadcasted_iota(jnp.int32, (8, 128), 0)
    lane = lax.broadcasted_iota(jnp.int32, (8, 128), 1)
    row = pivot
    if follow:
        l, c2, nxt = follow
    for j in range(8):
        d = row_of(c[j], j)
        inv = 1.0 / d
        scale = lax.rsqrt(d)
        here, unit = sub == j, lane == s + j
        m = jnp.where(here, -inv, c[j] * inv)
        pivot = jnp.where(unit, jnp.where(here, 1.0, 0.0), pivot)
        q = row_of(pivot, j)
        row = jnp.where(here, q * scale, row)
        pivot = jnp.where(here, 0.0, pivot) - m * q
        heads = {k: row_of(c[k], j) for k in range(j + 1, 8)}
        for k in range(j + 1, 8):
            c[k] = jnp.where(here, 0.0, c[k]) - m * heads[k]
        if follow:
            ml = l[j] * inv
            nxt = jnp.where(unit, 0.0, nxt) - ml * q
            for k in range(8):
                c2[k] = c2[k] - ml * row_of(l[j], k)
            for k in range(j + 1, 8):
                l[k] = l[k] - ml * heads[k]
    return pivot, row, nxt if follow else None


def factor_block(a, beside):
    tiles = len(a)
    lane = lax.broadcasted_iota(jnp.int32, (8, 128), 1)
    rows = []
    for p in range(0, tiles, 2):
        s = 8 * p
        c = [lanes_of(a[p], s + j) for j in range(8)]
        l = [lanes_of(a[p + 1], s + j) for j in range(8)]
        c2 = [lanes_of(a[p + 1], s + 8 + j) for j in range(8)]
        far = p + 2 + NEAR
        near = range(p + 2, min(far, tiles))
        old = {i: [lanes_of(a[i], s + j) for j in range(16)] for i in near}
        q1, row, nxt = eliminate(c, a[p], s, (l, c2, a[p + 1]))
        rows.append(row)
        beside(p)
        u = [lanes_of(q1, s + 8 + j) for j in range(8)]
        q2, row, _ = eliminate(c2, nxt, s + 8)
        rows.append(row)
        beside(p + 1)
        if p + 2 == tiles:
            break
        heads = [row_of(q2, j) for j in range(8)]
        q1 = jnp.where((lane >= s + 8) & (lane < s + 16), 0.0, q1) - tree_sum([u[j] * heads[j] for j in range(8)])
        band = (lane >= s) & (lane < s + 16)
        if far < tiles:
            left = jnp.concatenate([a[i][:, s : s + 16] for i in range(far, tiles)], axis=0)
            prod = jnp.dot(left, jnp.concatenate([q1, q2], axis=0), precision=HI, preferred_element_type=F32)
        heads = [row_of(q1, j) for j in range(8)] + heads
        for i in near:
            a[i] = jnp.where(band, 0.0, a[i]) - tree_sum([old[i][j] * heads[j] for j in range(16)])
        for i in range(far, tiles):
            at = 8 * (i - far)
            a[i] = jnp.where(band, 0.0, a[i]) - prod[at : at + 8, :]
    return rows


def chol_kernel(g_ref, w_hbm, modes_ref, r_ref, work, w_ref, inv, stage, r_rows, sem, w_sem, r_sem, last_sem):
    n = r_ref.shape[1]
    blocks = n // 128
    rows = w_ref.shape[0]
    piece = rows // 16
    bring = pltpu.make_async_copy(w_hbm, w_ref, w_sem)
    bring.start()
    sub = lax.broadcasted_iota(jnp.int32, (8, 128), 0)
    lane = lax.broadcasted_iota(jnp.int32, (8, 128), 1)
    NT = (((1,), (1,)), ((), ()))
    order = [(i, j) for i in range(blocks) for j in range(i, blocks)]

    def cols(j, count=1):
        return pl.ds(j * 128, count * 128)

    for index, (i, j) in enumerate(order):
        work[cols(i), cols(j)] = g_ref[cols(index), :]
    for i in range(1, blocks):
        work[cols(i), cols(blocks, i)] = jnp.zeros((128, i * 128), F32)

    def finish(kb, window):
        work[cols(kb), window] = jnp.dot(
            work[cols(kb), cols(kb + blocks)], work[cols(kb), window], precision=HI, preferred_element_type=F32
        )

    def update(kb, i, window):
        left = work[cols(kb), cols(i)].T
        work[cols(i), window] = work[cols(i), window] - jnp.dot(
            left, work[cols(kb), window], precision=HI, preferred_element_type=F32
        )

    def keep(kb):
        depth = (kb + 1) * 128
        row = work[cols(kb), pl.ds(n, depth)]
        high = row.astype(BF)
        inv[kb % 2, 0:128, 0:depth] = high
        inv[kb % 2, 128:256, 0:depth] = (row - high.astype(F32)).astype(BF)
        if kb > 0:
            r_rows[cols(kb), cols(0, kb)] = jnp.zeros((128, kb * 128), F32)
        if kb + 1 < blocks:
            r_rows[cols(kb), cols(kb + 1, blocks - kb - 1)] = work[cols(kb), cols(kb + 1, blocks - kb - 1)]
        r_copy(kb).start()

    def product(kb, first, count):
        depth = (kb + 1) * 128
        x = w_ref[pl.ds(first, count), 0:depth]
        both = lax.dot_general(x, inv[kb % 2, :, 0:depth], NT, preferred_element_type=F32)
        stage[kb % 2, pl.ds(first, count), :] = both[:, 0:128] + both[:, 128:256]

    def out_copy(kb, part):
        here = pl.ds(part * rows // 2, rows // 2)
        return pltpu.make_async_copy(
            stage.at[kb % 2, here, :], modes_ref.at[here, cols(kb)], sem.at[kb % 2, part]
        )

    def r_copy(kb):
        return pltpu.make_async_copy(r_rows.at[cols(kb), :], r_ref.at[cols(kb), :], r_sem.at[kb])

    for kb in range(blocks):
        waiting = []
        if kb >= 1:
            prev = kb - 1
            waiting = [
                [functools.partial(finish, prev, pl.ds((prev + 2) * 128, n - 256))],
                [functools.partial(keep, prev)],
                [functools.partial(update, prev, kb, pl.ds((kb + 1) * 128, n - 128))],
            ]
            for i in range(kb + 1, blocks):
                waiting.append([functools.partial(update, prev, i, pl.ds(i * 128, n + (kb - i) * 128))])
            waiting += [[] for _ in range(16 - len(waiting))]
            for q in range(16):
                waiting[min(q + 2, 15 - q % 2)].append(functools.partial(product, prev, q * piece, piece))
            waiting[10].append(lambda prev=prev: out_copy(prev, 0).start())

        def beside(p):
            if waiting:
                for task in waiting[p]:
                    task()

        if kb == 1:
            bring.wait()
        if kb >= 3:
            for part in range(2):
                out_copy(kb - 3, part).wait()
        a = [work[pl.ds(kb * 128 + 8 * i, 8), cols(kb)] for i in range(16)]
        for i, row in enumerate(factor_block(a, beside)):
            here = pl.ds(kb * 128 + 8 * i, 8)
            diagonal, left = lane == sub + 8 * i, lane <= sub + 8 * i
            r_rows[here, cols(kb)] = jnp.where(left, jnp.where(diagonal, 1.0 / row, 0.0), row)
            work[here, cols(kb + blocks)] = jnp.where(left, row, 0.0)
        if kb >= 1:
            out_copy(kb - 1, 1).start()
        if kb + 1 < blocks:
            finish(kb, cols(kb + 1))
            update(kb, kb + 1, cols(kb + 1))
        else:
            finish(kb, cols(kb + 1, blocks - 1))
            keep(kb)

    kb = blocks - 1
    for part in range(2):
        out_copy(kb - 2, part).wait()
    chunk = rows // 8

    def last_copy(q):
        part = pl.ds(pl.multiple_of(q * chunk, chunk), chunk)
        return pltpu.make_async_copy(stage.at[kb % 2, part, :], modes_ref.at[part, cols(kb)], last_sem.at[q])

    for q in range(8):
        product(kb, q * chunk, chunk)
        last_copy(q).start()

    @pl.loop(0, 8)
    def _(q):
        last_copy(q).wait()

    for part in range(2):
        out_copy(kb - 1, part).wait()
    for i in range(blocks):
        r_copy(i).wait()


def factor_and_modes(gram, weighted):
    rows, n = weighted.shape
    vm = pl.BlockSpec(memory_space=pltpu.VMEM)
    anyspace = pl.BlockSpec(memory_space=pl.ANY)
    return pl.pallas_call(
        chol_kernel,
        name="factor_modes",
        out_shape=(jax.ShapeDtypeStruct((rows, n), F32), jax.ShapeDtypeStruct((n, n), F32)),
        in_specs=[vm, anyspace],
        out_specs=(anyspace, anyspace),
        scratch_shapes=[
            pltpu.VMEM((n, 2 * n), F32),
            pltpu.VMEM((rows, n), BF),
            pltpu.VMEM((2, 256, n), BF),
            pltpu.VMEM((2, rows, 128), F32),
            pltpu.VMEM((n, n), F32),
            pltpu.SemaphoreType.DMA((2, 2)),
            pltpu.SemaphoreType.DMA(()),
            pltpu.SemaphoreType.DMA((n // 128,)),
            pltpu.SemaphoreType.DMA((8,)),
        ],
        compiler_params=pltpu.CompilerParams(),
    )(gram, weighted)


def on_device(snapshots, lift, adjacency, codes, obstacle):
    weighted, gram = weigh_and_gram(snapshots, lift, adjacency, codes, obstacle)
    return factor_and_modes(gram, weighted)


def solution(mesh):
    split = Mesh(
        mesh.devices.reshape(4, 4, 2, mesh.shape["tm"]), ("rows_0", "rows_1", "rows_2", "tm")
    )
    return jax.shard_map(
        on_device,
        mesh=split,
        in_specs=(P(ROWS, "tm"), P(), P(ROWS_TM, None), P(ROWS_TM, None), P(ROWS_TM)),
        out_specs=(P(ROWS_TM, None), P()),
        check_vma=False,
    )
```
